256 devices in a mesh: seq: 16 (over x_hi, y, core), heads: 16 (over z, x_lo).
Axes of the slice: x: 4 (x_hi: 2, x_lo: 2; x = x_hi * 2 + x_lo), y: 4, z: 8, core: 2. Of those that a mesh axis runs over, the one named last changes fastest.
Arguments:
- activations: bfloat16 [12288, 4096], P('seq', 'heads'), may hold values from -24 to 24
- w_query: bfloat16 [4096, 4096], P(None, 'heads'), may hold values from -0.1875 to 0.1875
- w_key: bfloat16 [4096, 4096], P(None, 'heads'), may hold values from -0.09375 to 0.09375
- w_value: bfloat16 [4096, 4096], P(None, 'heads'), may hold values from -0.09375 to 0.09375
- w_out: bfloat16 [4096, 4096], P('heads'), may hold values from -0.1875 to 0.1875
- windows: int32 [32], P('heads'), may hold values from 1 to 2, as said below
- rand_blocks: int32 [96, 3], P('seq'), may hold values from 0 to 95, as said below
- global_pos: int32 [128], replicated, may hold values from 0 to 12287, as said below
Outputs:
- attended: bfloat16 [12288, 4096], P('seq', 'heads')
The draws below stay inside these ranges and needn't reach their ends.
Inputs may be any that keep to these rules, and one draw needn't show every extreme that they name: `windows`: some head has reach 2. `rand_blocks`: the 3 entries of a row are distinct. Of the 18 entries in the rows of one index of seq, at most 2 fall into the 6 blocks of any one index, and exactly 2 into those of some index. `global_pos`: Distinct. At most 32 fall into the 768 positions of one index of seq, and exactly 32 into those of some index.
All inputs are finite; a program needn't handle non-finite values.
Results may differ from the reference program's by a relative error of at most 0.024.
The reference program's roundings to bfloat16 on the way count: a program that leaves them out, or rounds other values in their place, can miss the bound.
Values may be sent and summed in bfloat16 or wider, within the bound.
No kernel may reach another device: no remote copies, remote signals or barrier semaphores. Data moves between devices by JAX's collectives and lax.ppermute only.
A program may use at most 128 MiB of HBM per device.

```python
import math
import jax
import jax.numpy as jnp
from jax import lax

D = 4096
HEADS = 32
HD = 128
BLK = 128
BLK_DEV = 6
WMAX = 2
R = 3
G = 128
GMAX = 32
TOK_DEV = 768
SEQ = 12288
NBLK = 96
N_SEQ = 16
N_HEADS = 16


def draw_activations(key, part):
    first = jax.random.fold_in(key, 0)
    third = jax.random.fold_in(key, 2)
    direction = jnp.where(jax.random.uniform(third, (1, D), jnp.float32) < 0.5, -1.0, 1.0)
    place = (jnp.arange(SEQ, dtype=jnp.float32) / SEQ)[:, None]
    ramp = 0.3 + 1.7 * place
    values = jnp.clip(jax.random.normal(first, (SEQ, D), jnp.float32), -6.0, 6.0) + ramp * direction
    return values.astype(jnp.bfloat16)


def draw_windows(key, part):
    first, second = jax.random.split(key)
    widths = jax.random.randint(first, (HEADS,), 1, WMAX + 1)
    marked = jax.random.randint(second, (), 0, HEADS)
    return jnp.where(jnp.arange(HEADS) == marked, WMAX, widths).astype(jnp.int32)


def shuffle_sources(sub_key):
    return jax.random.permutation(sub_key, N_SEQ)


def shuffle_offsets(sub_key):
    return jax.random.permutation(sub_key, TOK_DEV)


def draw_rand_blocks(key, part):
    first, second = jax.random.split(key)
    orders = jax.vmap(shuffle_sources)(jax.random.split(first, N_SEQ))
    slot_index = jnp.arange(BLK_DEV * R) % N_SEQ
    sources = orders[:, slot_index]
    inner = jax.random.randint(second, (N_SEQ, BLK_DEV * R), 0, BLK_DEV)
    return (sources * BLK_DEV + inner).reshape(NBLK, R).astype(jnp.int32)


def draw_global_pos(key, part):
    first, second, third = jax.random.split(key, 3)
    crowded = jax.random.randint(first, (), 0, N_SEQ)
    number = jnp.arange(G)
    others = jnp.maximum(number - GMAX, 0)
    owners = jnp.where(number < GMAX, crowded, (crowded + 1 + others % (N_SEQ - 1)) % N_SEQ)
    ranks = jnp.where(number < GMAX, number, others // (N_SEQ - 1))
    offsets = jax.vmap(shuffle_offsets)(jax.random.split(second, N_SEQ))
    positions = owners * TOK_DEV + offsets[owners, ranks]
    order = jax.random.permutation(third, G)
    return positions[order].astype(jnp.int32)


def levels(rng, extent, shards, smallest, top_value):
    factor_of = 1.0
    for dim, shards_of in shards:
        steps = jax.random.uniform(jax.random.fold_in(jax.random.fold_in(rng, 6), dim), (shards_of,), jnp.float32, smallest / len(shards), top_value / len(shards))
        factor_of = factor_of * jnp.repeat(jnp.exp(steps), extent[dim] // shards_of).reshape((-1,) + (1,) * (len(extent) - 1 - dim))
    return factor_of


def normal_values(stream_key, shape, spread, limit, cuts=(), kind=jnp.bfloat16):
    values = spread * jax.random.normal(stream_key, shape, jnp.float32)
    if cuts:
        values = values * levels(stream_key, shape, cuts, -0.22, 0.18)
    return jnp.clip(values, -limit, limit).astype(kind)


def setup_inputs(seed: int = 0) -> dict:
    key_of = jax.random.split(jax.random.key(seed), 9)
    activations = draw_activations(jax.random.fold_in(key_of[8], 71), 0)
    w_query = normal_values(key_of[1], (D, HEADS * HD), (D // 4) ** -0.5, 0.1875, ((1, 16),))
    w_key = normal_values(key_of[2], (D, HEADS * HD), D ** -0.5, 0.09375, ((1, 16),))
    w_value = normal_values(key_of[3], (D, HEADS * HD), D ** -0.5, 0.09375, ((1, 16),))
    w_out = normal_values(key_of[4], (HEADS * HD, D), (HEADS * HD // 4) ** -0.5, 0.1875, ((0, 16),))
    windows = draw_windows(jax.random.fold_in(key_of[8], 71), 0)
    rand_blocks = draw_rand_blocks(jax.random.fold_in(key_of[8], 71), 0)
    global_pos = draw_global_pos(jax.random.fold_in(key_of[8], 71), 0)
    return dict(activations=activations, w_query=w_query, w_key=w_key, w_value=w_value, w_out=w_out, windows=windows, rand_blocks=rand_blocks, global_pos=global_pos)


NEGATIVE = -1e+30

def head_context(q_head, k_head, v_head, reach, rand_blocks, global_pos):
    score_scale = 1.0 / math.sqrt(HD)
    offsets = jnp.arange(2 * WMAX + 1, dtype=jnp.int32) - WMAX
    block_ids = jnp.arange(NBLK, dtype=jnp.int32)
    key_ids = jnp.concatenate([(block_ids[:, None] + offsets[None, :]) % NBLK, rand_blocks], axis=1)
    nearby_count = (2 * WMAX + 1 + R) * BLK
    q_float = q_head.astype(jnp.float32)
    k_float = k_head.astype(jnp.float32)
    v_float = v_head.astype(jnp.float32)
    k_blocks = k_float.reshape(NBLK, BLK, HD)
    v_blocks = v_float.reshape(NBLK, BLK, HD)
    nearby_keys = k_blocks[key_ids].reshape(NBLK, nearby_count, HD)
    nearby_values = v_blocks[key_ids].reshape(NBLK, nearby_count, HD)
    global_key_rows = k_float[global_pos]
    global_value_rows = v_float[global_pos]
    query_blocks = q_float.reshape(NBLK, BLK, HD)
    nearby_scores = jnp.einsum('lns,ljs->lnj', query_blocks, nearby_keys) * score_scale
    global_score_rows = jnp.einsum('wes,js->wej', query_blocks, global_key_rows) * score_scale
    window_valid = jnp.abs(offsets) <= reach
    valid = jnp.concatenate([jnp.repeat(window_valid, BLK), jnp.ones((R * BLK + G,), dtype=bool)])
    scores = jnp.concatenate([nearby_scores, global_score_rows], axis=-1)
    masked = jnp.where(valid, scores, NEGATIVE)
    highest = lax.optimization_barrier(jnp.max(masked, axis=-1, keepdims=True))
    probs = jnp.where(valid, jnp.exp(masked - highest), 0.0)
    total = lax.optimization_barrier(jnp.sum(probs, axis=-1, keepdims=True))
    attention_weights = lax.optimization_barrier(probs.astype(jnp.bfloat16)).astype(jnp.float32)
    numerator = jnp.einsum('lma,lap->lmp', attention_weights[..., :nearby_count], nearby_values)
    numerator = numerator + jnp.einsum('lft,to->lfo', attention_weights[..., nearby_count:], global_value_rows)
    context = (numerator / total).reshape(SEQ, HD)
    g_query = q_float[global_pos]
    g_scores = jnp.einsum('gd,td->gt', g_query, k_float) * score_scale
    g_high = lax.optimization_barrier(jnp.max(g_scores, axis=-1, keepdims=True))
    g_probs = jnp.exp(g_scores - g_high)
    g_total = lax.optimization_barrier(jnp.sum(g_probs, axis=-1, keepdims=True))
    g_weights = lax.optimization_barrier(g_probs.astype(jnp.bfloat16)).astype(jnp.float32)
    g_context = jnp.einsum('gt,td->gd', g_weights, v_float) / g_total
    return context.at[global_pos].set(g_context)

def reference(activations, w_query, w_key, w_value, w_out, windows, rand_blocks, global_pos):
    query = jnp.dot(activations, w_query, preferred_element_type=jnp.float32).astype(jnp.bfloat16)
    keys = jnp.dot(activations, w_key, preferred_element_type=jnp.float32).astype(jnp.bfloat16)
    values = jnp.dot(activations, w_value, preferred_element_type=jnp.float32).astype(jnp.bfloat16)
    q_heads = query.reshape(SEQ, HEADS, HD).transpose(1, 0, 2)
    k_heads = keys.reshape(SEQ, HEADS, HD).transpose(1, 0, 2)
    v_heads = values.reshape(SEQ, HEADS, HD).transpose(1, 0, 2)

    def one_head(inputs):
        q_head, k_head, v_head, reach = inputs
        return head_context(q_head, k_head, v_head, reach, rand_blocks, global_pos)
    contexts = lax.map(one_head, (q_heads, k_heads, v_heads, windows))
    ctx = contexts.transpose(1, 0, 2).reshape(SEQ, HEADS * HD).astype(jnp.bfloat16)
    group_width = HEADS // N_HEADS * HD
    ctx_groups = ctx.reshape(SEQ, N_HEADS, group_width)
    w_groups = w_out.reshape(N_HEADS, group_width, D)

    def add_group(running, group):
        block_ctx = lax.dynamic_index_in_dim(ctx_groups, group, 1, keepdims=False)
        block_w = lax.dynamic_index_in_dim(w_groups, group, 0, keepdims=False)
        part = jnp.dot(block_ctx, block_w, preferred_element_type=jnp.float32).astype(jnp.bfloat16)
        part = lax.optimization_barrier(part)
        return (running + part.astype(jnp.float32), None)
    summed, _ = lax.scan(add_group, jnp.zeros((SEQ, D), jnp.float32), jnp.arange(N_HEADS, dtype=jnp.int32))
    return summed.astype(jnp.bfloat16)
```

```python
import math

import jax
import jax.numpy as jnp
from jax import lax
from jax.experimental import pallas as pl
from jax.experimental.pallas import tpu as pltpu
from jax.sharding import PartitionSpec as P

WMAX = 2
SPAN = 2 * WMAX + 1
R = 3
PICKS = SPAN + R
BLK = 128
BLK_DEV = 6
ROWS = BLK * BLK_DEV
GMAX = 32
G = 128
HD = 128
HEADS_DEV = 2
WIDTH = HD * HEADS_DEV
N_SEQ = 16
N_HEADS = 16
NBLK = N_SEQ * BLK_DEV
UNIT = ROWS + GMAX
NEGATIVE = -1e30
SCALE = 1.0 / math.sqrt(HD)
F32 = jnp.float32
BF16 = jnp.bfloat16

HEAD_SLOTS = (
    ((0, 0), (0, 0), (0, 0)),
    ((-1, 0), (1, 0), (-1, 0)),
    ((-2, 0), (2, 0), (1, 0)),
    ((-3, 0), (1, 1), (-2, 0)),
    ((-2, 1), (2, 1), (-4, 0)),
)
Z_UP = [(h, (h + 2) % 16) for h in range(16)]
Z_DOWN = [(h, (h - 2) % 16) for h in range(16)]
PAIR = [(h, h ^ 1) for h in range(16)]


def head_order():
    items = [(0, 0)]
    for up, down, across in HEAD_SLOTS:
        items += [
            (up[0] - 1, up[1]),
            (down[0] + 1, down[1]),
            (across[0], across[1] ^ 1),
        ]
    return items


Y_UP = [(s, (s // 8) * 8 + (s % 8 + 2) % 8) for s in range(16)]
Y_DOWN = [(s, (s // 8) * 8 + (s % 8 - 2) % 8) for s in range(16)]
HALF = [(s, s ^ 8) for s in range(16)]
CORE = [(s, s ^ 1) for s in range(16)]


def vmem():
    return pl.BlockSpec(memory_space=pltpu.VMEM)


def project_kernel(count, first, last, ids, *refs):
    xs, refs = refs[:count], refs[count:]
    ws, refs = refs[: 3 * count], refs[3 * count :]
    if not first:
        acc, refs = refs[0], refs[1:]
    if last:
        sel_ref, q_out, kv_out = refs
    else:
        (out,) = refs
    parts = []
    for j in range(3):
        total = None if first else acc[:, j * WIDTH : (j + 1) * WIDTH]
        for i in range(count):
            term = jnp.dot(
                xs[i][...], ws[3 * i + j][...], preferred_element_type=F32
            )
            total = term if total is None else total + term
        if last:
            parts.append(total.astype(BF16))
        else:
            out[:, j * WIDTH : (j + 1) * WIDTH] = total
    if last:
        columns = lax.broadcasted_iota(jnp.int32, (GMAX, ROWS), 1)
        pick = jnp.where(columns == sel_ref[...], 1.0, 0.0).astype(BF16)
        for j, part in enumerate(parts):
            chosen = jnp.dot(pick, part, preferred_element_type=F32).astype(BF16)
            dest = q_out if j == 0 else kv_out
            low = max(j - 1, 0) * WIDTH
            dest[:ROWS, low : low + WIDTH] = part
            dest[ROWS:, low : low + WIDTH] = chosen


def project(ids, offset, xs, weights, acc, selected=None):
    count = len(xs)
    first, last = acc is None, selected is not None
    full = lambda shape: pl.BlockSpec(shape, lambda g, ids: (0, 0))
    in_specs = [full((ROWS, WIDTH)) for _ in xs]
    operands = list(xs)
    for i in range(count):
        for w in weights:
            in_specs.append(
                pl.BlockSpec((WIDTH, WIDTH), lambda g, ids, i=i: (ids[offset + i], 0))
            )
            operands.append(w)
    aliases = {}
    if not first:
        in_specs.append(full((ROWS, 3 * WIDTH)))
        operands.append(acc)
        if not last:
            aliases = {len(operands): 0}
    if last:
        in_specs.append(full((GMAX, 1)))
        operands.append(selected)
        out_shape = (
            jax.ShapeDtypeStruct((UNIT, WIDTH), BF16),
            jax.ShapeDtypeStruct((UNIT, 2 * WIDTH), BF16),
        )
        out_specs = (full((UNIT, WIDTH)), full((UNIT, 2 * WIDTH)))
    else:
        out_shape = jax.ShapeDtypeStruct((ROWS, 3 * WIDTH), F32)
        out_specs = full((ROWS, 3 * WIDTH))

    def body(*refs):
        project_kernel(count, first, last, *refs)

    return pl.pallas_call(
        body,
        out_shape=out_shape,
        grid_spec=pltpu.PrefetchScalarGridSpec(
            num_scalar_prefetch=1, grid=(1,), in_specs=in_specs, out_specs=out_specs
        ),
        input_output_aliases=aliases,
        compiler_params=pltpu.CompilerParams(vmem_limit_bytes=40 << 20),
        cost_estimate=pl.CostEstimate(
            flops=2 * count * ROWS * WIDTH * 3 * WIDTH,
            transcendentals=0,
            bytes_accessed=6 << 20,
        ),
        name="project",
    )(ids, *operands)


def combine_kernel(count, first, last, ids, *refs):
    cs, refs = refs[:count], refs[count:]
    ws, refs = refs[:count], refs[count:]
    total = None
    if not first:
        acc, refs = refs[0], refs[1:]
        total = acc[...]
    (out,) = refs
    for i in range(count):
        part = jnp.dot(cs[i][...], ws[i][0], preferred_element_type=F32)
        part = part.astype(BF16).astype(F32)
        total = part if total is None else total + part
    out[...] = total.astype(out.dtype)


def combine(ids, offset, cs, w_parts, acc, last=False):
    count = len(cs)
    first = acc is None
    full = lambda shape: pl.BlockSpec(shape, lambda g, ids: (0, 0))
    in_specs = [full((ROWS, WIDTH)) for _ in cs]
    operands = list(cs)
    for i in range(count):
        in_specs.append(
            pl.BlockSpec(
                (1, WIDTH, WIDTH), lambda g, ids, i=i: (ids[offset + i], 0, 0)
            )
        )
        operands.append(w_parts)
    aliases = {}
    if not first:
        in_specs.append(full((ROWS, WIDTH)))
        operands.append(acc)
        if not last:
            aliases = {len(operands): 0}

    def body(*refs):
        combine_kernel(count, first, last, *refs)

    return pl.pallas_call(
        body,
        out_shape=jax.ShapeDtypeStruct((ROWS, WIDTH), BF16 if last else F32),
        grid_spec=pltpu.PrefetchScalarGridSpec(
            num_scalar_prefetch=1,
            grid=(1,),
            in_specs=in_specs,
            out_specs=full((ROWS, WIDTH)),
        ),
        input_output_aliases=aliases,
        compiler_params=pltpu.CompilerParams(vmem_limit_bytes=40 << 20),
        cost_estimate=pl.CostEstimate(
            flops=2 * count * ROWS * WIDTH * WIDTH,
            transcendentals=0,
            bytes_accessed=3 << 20,
        ),
        name="combine",
    )(ids, *operands)


def gather_heads(own):
    have = {(0, 0): own}
    for up, down, across in HEAD_SLOTS:
        got = [
            lax.ppermute(have[up], "heads", Z_UP),
            lax.ppermute(have[down], "heads", Z_DOWN),
            lax.ppermute(have[across], "heads", PAIR),
        ]
        have[(up[0] - 1, up[1])] = got[0]
        have[(down[0] + 1, down[1])] = got[1]
        have[(across[0], across[1] ^ 1)] = got[2]
        yield got


def gather_seq(own):
    up = lambda a: lax.ppermute(a, "seq", Y_UP)
    down = lambda a: lax.ppermute(a, "seq", Y_DOWN)
    half = lambda a: lax.ppermute(a, "seq", HALF)
    have = {(0, 0): own}
    have[0, 3] = up(own)
    have[0, 1] = down(own)
    have[1, 0] = half(own)
    have[0, 2] = up(have[0, 3])
    have[1, 1] = down(have[1, 0])
    have[1, 3] = half(have[0, 3])
    pieces = [(dx * 8 + dy * 2, 0, piece) for (dx, dy), piece in have.items()]
    cuts = (0, 272, 544, UNIT)
    last = (
        up(lax.slice_in_dim(have[1, 3], cuts[0], cuts[1], axis=0)),
        down(lax.slice_in_dim(have[1, 1], cuts[1], cuts[2], axis=0)),
        half(lax.slice_in_dim(have[0, 2], cuts[2], cuts[3], axis=0)),
    )
    for i, piece in enumerate(last):
        pieces.append((12, cuts[i], piece))
    pieces += [
        (slot + 1, row, lax.ppermute(piece, "seq", CORE)) for slot, row, piece in pieces
    ]
    return pieces


def attention_kernel(layout, slots, rows, windows, q_ref, gslot_ref, sel_ref, *refs):
    count = len(layout)
    pieces, (out_ref, buf, sems) = refs[:count], refs[count:]
    copies = []
    for i, (slot, row) in enumerate(layout):
        size = pieces[i].shape[0]
        copies.append(
            pltpu.make_async_copy(
                pieces[i], buf.at[slot, pl.ds(row, size)], sems.at[i]
            )
        )
    for copy in copies:
        copy.start()
    for copy in copies:
        copy.wait()

    dims = (((1,), (1,)), ((), ()))
    found = jnp.concatenate([buf[i, ROWS:UNIT, :] for i in range(N_SEQ)], axis=0)
    where = lax.broadcasted_iota(jnp.int32, (G, N_SEQ * GMAX), 1)
    pick = jnp.where(where == gslot_ref[...], 1.0, 0.0).astype(BF16)
    g_kv = jnp.dot(pick, found, preferred_element_type=F32).astype(BF16)

    steps = lax.broadcasted_iota(jnp.int32, (ROWS, GMAX), 0)
    place = jnp.where(steps == sel_ref[...], 1.0, 0.0)
    is_global = jnp.sum(place, axis=1, keepdims=True) > 0.5
    place = place.astype(BF16)

    for head in range(HEADS_DEV):
        low, high = head * HD, (head + 1) * HD
        vlow, vhigh = WIDTH + low, WIDTH + high
        g_query = q_ref[ROWS:UNIT, low:high]
        g_scores = [
            lax.dot_general(
                g_query, buf[i, :ROWS, low:high], dims, preferred_element_type=F32
            )
            * SCALE
            for i in range(N_SEQ)
        ]
        top = g_scores[0]
        for s in g_scores[1:]:
            top = jnp.maximum(top, s)
        top = jnp.max(top, axis=1, keepdims=True)
        sums = jnp.zeros((GMAX, ROWS), F32)
        acc = jnp.zeros((GMAX, HD), F32)
        for i in range(N_SEQ):
            p = jnp.exp(g_scores[i] - top)
            sums = sums + p
            acc = acc + jnp.dot(
                p.astype(BF16), buf[i, :ROWS, vlow:vhigh], preferred_element_type=F32
            )
        total = jnp.sum(sums, axis=1, keepdims=True)
        g_context = (acc / total).astype(BF16)
        placed = jnp.dot(place, g_context, preferred_element_type=F32)
        wide = windows[head] >= WMAX
        for b in range(BLK_DEV):
            query = q_ref[b * BLK : (b + 1) * BLK, low:high]
            where_kv = [
                (slots[b * PICKS + j], pl.multiple_of(rows[b * PICKS + j], BLK))
                for j in range(PICKS)
            ]
            scores = []
            for j, (slot, row) in enumerate(where_kv):
                s = (
                    lax.dot_general(
                        query,
                        buf[slot, pl.ds(row, BLK), low:high],
                        dims,
                        preferred_element_type=F32,
                    )
                    * SCALE
                )
                if j == 0 or j == SPAN - 1:
                    s = jnp.where(wide, s, NEGATIVE)
                scores.append(s)
            scores.append(
                lax.dot_general(
                    query, g_kv[:, low:high], dims, preferred_element_type=F32
                )
                * SCALE
            )
            top = scores[0]
            for s in scores[1:]:
                top = jnp.maximum(top, s)
            top = jnp.max(top, axis=1, keepdims=True)
            sums = None
            acc = None
            for j, s in enumerate(scores):
                p = jnp.exp(s - top)
                sums = p if sums is None else sums + p
                if j < PICKS:
                    slot, row = where_kv[j]
                    v = buf[slot, pl.ds(row, BLK), vlow:vhigh]
                else:
                    v = g_kv[:, vlow:vhigh]
                term = jnp.dot(p.astype(BF16), v, preferred_element_type=F32)
                acc = term if acc is None else acc + term
            context = acc / jnp.sum(sums, axis=1, keepdims=True)
            span = slice(b * BLK, (b + 1) * BLK)
            out_ref[span, low:high] = jnp.where(
                is_global[span], placed[span], context
            ).astype(BF16)


def attention(slots, rows, windows, query, gslot, selected, pieces):
    layout = [(slot, row) for slot, row, _ in pieces]
    smem_blocks = [vmem()] * 3 + [pl.BlockSpec(memory_space=pl.ANY)] * len(pieces)

    def body(*refs):
        attention_kernel(layout, *refs)

    return pl.pallas_call(
        body,
        out_shape=jax.ShapeDtypeStruct((ROWS, WIDTH), BF16),
        grid_spec=pltpu.PrefetchScalarGridSpec(
            num_scalar_prefetch=3,
            grid=(),
            in_specs=smem_blocks,
            out_specs=vmem(),
            scratch_shapes=[
                pltpu.VMEM((N_SEQ, UNIT, 2 * WIDTH), BF16),
                pltpu.SemaphoreType.DMA((len(pieces),)),
            ],
        ),
        compiler_params=pltpu.CompilerParams(vmem_limit_bytes=48 << 20),
        cost_estimate=pl.CostEstimate(
            flops=2 << 30, transcendentals=3 << 20, bytes_accessed=14 << 20
        ),
        name="attention",
    )(slots, rows, windows, query, gslot, selected, *[p for _, _, p in pieces])


def on_device(
    activations, w_query, w_key, w_value, w_out, windows, rand_blocks, global_pos
):
    me = lax.axis_index("heads")
    here = lax.axis_index("seq")
    items = head_order()
    shifts = jnp.array([d for d, _ in items], jnp.int32)
    flips = jnp.array([e for _, e in items], jnp.int32)
    ids = (me // 2 + shifts + 8) % 8 * 2 + (me % 2 + flips) % 2

    def slot_of(seq):
        dx = (seq // 8 + here // 8) % 2
        dy = (seq // 2 % 4 - here // 2 % 4 + 4) % 4
        return dx * 8 + dy * 2 + (seq + here) % 2

    blocks = jnp.arange(BLK_DEV, dtype=jnp.int32)[:, None] + here * BLK_DEV
    offsets = jnp.arange(SPAN, dtype=jnp.int32)[None, :] - WMAX
    near = (blocks + offsets + NBLK) % NBLK
    named = jnp.concatenate([near, rand_blocks], axis=1).reshape(-1)
    key_slots = slot_of(named // BLK_DEV)
    key_rows = named % BLK_DEV * BLK

    owners = global_pos // ROWS
    order = jnp.arange(G, dtype=jnp.int32)
    earlier = (owners[:, None] == owners[None, :]) & (order[None, :] < order[:, None])
    ranks = jnp.sum(earlier.astype(jnp.int32), axis=1)
    gslot = (slot_of(owners) * GMAX + ranks)[:, None]
    mine = (owners == here)[None, :] & (
        ranks[None, :] == jnp.arange(GMAX, dtype=jnp.int32)[:, None]
    )
    selected = jnp.max(jnp.where(mine, (global_pos - here * ROWS)[None, :], -1), axis=1)

    weights = (w_query, w_key, w_value)
    acc = project(ids, 0, [activations], weights, None)
    slots = list(gather_heads(activations))
    for t, got in enumerate(slots[:-1]):
        acc = project(ids, 1 + 3 * t, got, weights, acc)
    query, unit = project(
        ids, 13, slots[-1], weights, acc, selected=selected[:, None]
    )

    w_blocks = w_out.reshape(WIDTH, N_HEADS, WIDTH).transpose(1, 0, 2)
    w_blocks, unit = lax.optimization_barrier((w_blocks, unit))
    pieces = gather_seq(unit)
    w_parts = lax.all_to_all(w_blocks, "heads", 0, 0)

    ctx = attention(
        key_slots, key_rows, windows, query, gslot, selected[None, :], pieces
    )
    out = combine(ids, 0, [ctx], w_parts, None)
    slots = list(gather_heads(ctx))
    for t, got in enumerate(slots):
        out = combine(ids, 1 + 3 * t, got, w_parts, out, last=t == len(slots) - 1)
    return out


def solution(mesh):
    in_specs = (
        P("seq", "heads"),
        P(None, "heads"),
        P(None, "heads"),
        P(None, "heads"),
        P("heads", None),
        P("heads"),
        P("seq", None),
        P(),
    )
    out_specs = P("seq", "heads")
    return jax.shard_map(
        on_device, mesh=mesh, in_specs=in_specs, out_specs=out_specs, check_vma=False
    )
```

```python
import math

import jax
import jax.numpy as jnp
from jax import lax
from jax.experimental import pallas as pl
from jax.experimental.pallas import tpu as pltpu
from jax.sharding import PartitionSpec as P

WMAX = 2
SPAN = 2 * WMAX + 1
R = 3
PICKS = SPAN + R
BLK = 128
BLK_DEV = 6
ROWS = BLK * BLK_DEV
GMAX = 32
G = 128
HD = 128
HEADS_DEV = 2
WIDTH = HD * HEADS_DEV
N_SEQ = 16
N_HEADS = 16
NBLK = N_SEQ * BLK_DEV
UNIT = ROWS + GMAX
NEGATIVE = -1e30
SCALE = 1.0 / math.sqrt(HD)
F32 = jnp.float32
BF16 = jnp.bfloat16

HEAD_SLOTS = (
    ((0, 0), (0, 0), (0, 0)),
    ((-1, 0), (1, 0), (-1, 0)),
    ((-2, 0), (2, 0), (1, 0)),
    ((-3, 0), (1, 1), (-2, 0)),
    ((-2, 1), (2, 1), (-4, 0)),
)
Z_UP = [(h, (h + 2) % 16) for h in range(16)]
Z_DOWN = [(h, (h - 2) % 16) for h in range(16)]
PAIR = [(h, h ^ 1) for h in range(16)]


def head_order():
    items = [(0, 0)]
    for up, down, across in HEAD_SLOTS:
        items += [
            (up[0] - 1, up[1]),
            (down[0] + 1, down[1]),
            (across[0], across[1] ^ 1),
        ]
    return items


Y_UP = [(s, (s // 8) * 8 + (s % 8 + 2) % 8) for s in range(16)]
Y_DOWN = [(s, (s // 8) * 8 + (s % 8 - 2) % 8) for s in range(16)]
HALF = [(s, s ^ 8) for s in range(16)]
CORE = [(s, s ^ 1) for s in range(16)]
Y_PAIR = [(s, s ^ 2) for s in range(16)]


def vmem():
    return pl.BlockSpec(memory_space=pltpu.VMEM)


def in_hbm(array):
    return pltpu.with_memory_space_constraint(array, pltpu.HBM)


def project_kernel(count, first, last, ids, core, *refs):
    xs, refs = refs[:count], refs[count:]
    ws, refs = refs[: 3 * count], refs[3 * count :]
    if not first:
        acc, refs = refs[0], refs[1:]
    if last:
        sel_ref, *outs = refs
    else:
        (out,) = refs
    parts = []
    for j in range(3):
        total = None if first else acc[:, j * WIDTH : (j + 1) * WIDTH]
        for i in range(count):
            term = jnp.dot(
                xs[i][...], ws[3 * i + j][...], preferred_element_type=F32
            )
            total = term if total is None else total + term
        if last:
            parts.append(total.astype(BF16))
        else:
            out[:, j * WIDTH : (j + 1) * WIDTH] = total
    if last:
        columns = lax.broadcasted_iota(jnp.int32, (GMAX, ROWS), 1)
        pick = jnp.where(columns == sel_ref[...], 1.0, 0.0).astype(BF16)
        second = core[0] > 0
        for j, part in enumerate(parts):
            chosen = jnp.dot(pick, part, preferred_element_type=F32).astype(BF16)
            low = max(j - 1, 0) * HD
            for rows, have in ((slice(0, ROWS), part), (slice(ROWS, UNIT), chosen)):
                left, right = have[:, :HD], have[:, HD:]
                q_or_kv = outs[:2] if j == 0 else outs[2:]
                q_or_kv[0][rows, low : low + HD] = jnp.where(second, right, left)
                q_or_kv[1][rows, low : low + HD] = jnp.where(second, left, right)


def project(ids, core, offset, xs, weights, acc, selected=None):
    count = len(xs)
    first, last = acc is None, selected is not None
    full = lambda shape: pl.BlockSpec(shape, lambda g, ids, core: (0, 0))
    in_specs = [full((ROWS, WIDTH)) for _ in xs]
    operands = list(xs)
    for i in range(count):
        for w in weights:
            in_specs.append(
                pl.BlockSpec((WIDTH, WIDTH), lambda g, ids, core, i=i: (ids[offset + i], 0))
            )
            operands.append(in_hbm(w))
    aliases = {}
    if not first:
        in_specs.append(full((ROWS, 3 * WIDTH)))
        operands.append(acc)
        if not last:
            aliases = {len(operands) + 1: 0}
    if last:
        in_specs.append(full((GMAX, 1)))
        operands.append(selected)
        shapes = ((UNIT, HD),) * 2 + ((UNIT, 2 * HD),) * 2
        out_shape = tuple(jax.ShapeDtypeStruct(shape, BF16) for shape in shapes)
        out_specs = tuple(full(shape) for shape in shapes)
    else:
        out_shape = jax.ShapeDtypeStruct((ROWS, 3 * WIDTH), F32)
        out_specs = full((ROWS, 3 * WIDTH))

    def body(*refs):
        project_kernel(count, first, last, *refs)

    return pl.pallas_call(
        body,
        out_shape=out_shape,
        grid_spec=pltpu.PrefetchScalarGridSpec(
            num_scalar_prefetch=2, grid=(1,), in_specs=in_specs, out_specs=out_specs
        ),
        input_output_aliases=aliases,
        compiler_params=pltpu.CompilerParams(vmem_limit_bytes=40 << 20),
        cost_estimate=pl.CostEstimate(
            flops=2 * count * ROWS * WIDTH * 3 * WIDTH,
            transcendentals=0,
            bytes_accessed=6 << 20,
        ),
        name="project",
    )(ids, core, *operands)


def combine_kernel(count, first, last, ids, odd, *refs):
    cs, refs = refs[:count], refs[count:]
    ws, refs = refs[: 4 * count], refs[4 * count :]
    flip = odd[0] > 0
    total = None
    if not first:
        acc, refs = refs[0], refs[1:]
        total = acc[...]
    (out,) = refs
    for i in range(count):
        quarters = [w[0] for w in ws[4 * i : 4 * i + 4]]
        w = jnp.concatenate(
            [
                jnp.where(flip, quarters[n ^ 1], quarters[n])
                for n in range(4)
            ],
            axis=0,
        )
        part = jnp.dot(cs[i][...], w, preferred_element_type=F32)
        part = part.astype(BF16).astype(F32)
        total = part if total is None else total + part
    out[...] = total.astype(out.dtype)


def combine(ids, odd, offset, cs, w_parts, acc, last=False):
    count = len(cs)
    first = acc is None
    full = lambda shape: pl.BlockSpec(shape, lambda g, ids, odd: (0, 0))
    in_specs = [full((ROWS, WIDTH)) for _ in cs]
    operands = list(cs)
    for i in range(count):
        for w in w_parts:
            in_specs.append(
                pl.BlockSpec(
                    (1, WIDTH // 4, WIDTH),
                    lambda g, ids, odd, i=i: (ids[offset + i], 0, 0),
                )
            )
            operands.append(in_hbm(w))
    aliases = {}
    if not first:
        in_specs.append(full((ROWS, WIDTH)))
        operands.append(acc)
        if not last:
            aliases = {len(operands) + 1: 0}

    def body(*refs):
        combine_kernel(count, first, last, *refs)

    return pl.pallas_call(
        body,
        out_shape=jax.ShapeDtypeStruct((ROWS, WIDTH), BF16 if last else F32),
        grid_spec=pltpu.PrefetchScalarGridSpec(
            num_scalar_prefetch=2,
            grid=(1,),
            in_specs=in_specs,
            out_specs=full((ROWS, WIDTH)),
        ),
        input_output_aliases=aliases,
        compiler_params=pltpu.CompilerParams(vmem_limit_bytes=40 << 20),
        cost_estimate=pl.CostEstimate(
            flops=2 * count * ROWS * WIDTH * WIDTH,
            transcendentals=0,
            bytes_accessed=3 << 20,
        ),
        name="combine",
    )(ids, odd, *operands)


def split_kernel(quarter, w_ref, out_ref):
    for j in range(N_HEADS):
        out_ref[j] = w_ref[:, j * WIDTH : (j + 1) * WIDTH]


def split_columns(quarter, w_out):
    rows = WIDTH // 4
    return pl.pallas_call(
        split_kernel,
        out_shape=jax.ShapeDtypeStruct((N_HEADS, rows, WIDTH), BF16),
        grid_spec=pltpu.PrefetchScalarGridSpec(
            num_scalar_prefetch=1,
            grid=(1,),
            in_specs=[
                pl.BlockSpec(
                    (rows, N_HEADS * WIDTH), lambda g, quarter: (quarter[0], 0)
                )
            ],
            out_specs=pl.BlockSpec(
                (N_HEADS, rows, WIDTH), lambda g, quarter: (0, 0, 0)
            ),
        ),
        cost_estimate=pl.CostEstimate(
            flops=0, transcendentals=0, bytes_accessed=1 << 20
        ),
        name="split_columns",
    )(quarter, in_hbm(w_out))


def gather_heads(own, work):
    have = {(0, 0): own}
    before = [own]
    for t, (up, down, across) in enumerate(HEAD_SLOTS):
        got = [
            lax.ppermute(have[up], "heads", Z_UP),
            lax.ppermute(have[down], "heads", Z_DOWN),
            lax.ppermute(have[across], "heads", PAIR),
        ]
        got, work.state = lax.optimization_barrier((got, work(t, before)))
        have[(up[0] - 1, up[1])] = got[0]
        have[(down[0] + 1, down[1])] = got[1]
        have[(across[0], across[1] ^ 1)] = got[2]
        before = got
    return before


def gather_seq(mine, theirs):
    up = lambda a: lax.ppermute(a, "seq", Y_UP)
    down = lambda a: lax.ppermute(a, "seq", Y_DOWN)
    half = lambda a: lax.ppermute(a, "seq", HALF)
    near = ({(0, 0): mine}, {(0, 0): theirs})
    first = ((0, 3), (0, 1), (1, 0))
    got = [(up(n[0, 0]), down(n[0, 0]), half(n[0, 0])) for n in near]
    for n, g in zip(near, lax.optimization_barrier(got)):
        n.update(zip(first, g))
    second = ((0, 2), (1, 1), (1, 3))
    got = [(up(n[0, 3]), down(n[1, 0]), half(n[0, 3])) for n in near]
    for n, g in zip(near, lax.optimization_barrier(got)):
        n.update(zip(second, g))
    near[0][1, 2] = up(near[0][1, 3])
    near[1][1, 2] = down(near[1][1, 1])
    return [near[slot % 2][slot // 8, slot // 2 % 4] for slot in range(N_SEQ)]


def attention_kernel(slots, rows, reach, *refs):
    queries, (gslot_ref, *sels), refs = refs[:2], refs[2:5], refs[5:]
    pieces, (*outs, buf, sems) = refs[:N_SEQ], refs[N_SEQ:]
    copies = [
        pltpu.make_async_copy(pieces[i], buf.at[i], sems.at[i]) for i in range(N_SEQ)
    ]
    for copy in copies:
        copy.start()
    for copy in copies:
        copy.wait()

    dims = (((1,), (1,)), ((), ()))

    def scored(q, k):
        return lax.dot_general(q, k, dims, preferred_element_type=F32) * SCALE

    found = jnp.concatenate([buf[i, ROWS:UNIT, :] for i in range(N_SEQ)], axis=0)
    where = lax.broadcasted_iota(jnp.int32, (G, N_SEQ * GMAX), 1)
    pick = jnp.where(where == gslot_ref[...], 1.0, 0.0).astype(BF16)
    g_kv = jnp.dot(pick, found, preferred_element_type=F32).astype(BF16)

    g_query = jnp.concatenate([q[ROWS:UNIT, :] for q in queries], axis=0)
    g_scores = [scored(g_query, buf[i, :ROWS, :HD]) for i in range(N_SEQ)]
    top = g_scores[0]
    for s in g_scores[1:]:
        top = jnp.maximum(top, s)
    top = jnp.max(top, axis=1, keepdims=True)
    sums = jnp.zeros((2 * GMAX, ROWS), F32)
    acc = jnp.zeros((2 * GMAX, HD), F32)
    for i in range(N_SEQ):
        p = jnp.exp(g_scores[i] - top)
        sums = sums + p
        acc = acc + jnp.dot(
            p.astype(BF16), buf[i, :ROWS, HD:], preferred_element_type=F32
        )
    g_context = (acc / jnp.sum(sums, axis=1, keepdims=True)).astype(BF16)

    wide = reach[0] >= WMAX
    for side in range(2):
        steps = lax.broadcasted_iota(jnp.int32, (ROWS, GMAX), 0)
        place = jnp.where(steps == sels[side][...], 1.0, 0.0)
        is_global = jnp.sum(place, axis=1, keepdims=True) > 0.5
        placed = jnp.dot(
            place.astype(BF16),
            g_context[side * GMAX : (side + 1) * GMAX],
            preferred_element_type=F32,
        )
        for b in range(BLK_DEV):
            span = slice(b * BLK, (b + 1) * BLK)
            query = queries[side][span, :]
            first = (side * BLK_DEV + b) * PICKS
            keys_at = [
                (slots[first + j], pl.ds(pl.multiple_of(rows[first + j], BLK), BLK))
                for j in range(PICKS)
            ]
            scores = [scored(query, buf[slot, at, :HD]) for slot, at in keys_at]
            for j in (0, SPAN - 1):
                scores[j] = jnp.where(wide, scores[j], NEGATIVE)
            scores.append(scored(query, g_kv[:, :HD]))
            top = scores[0]
            for s in scores[1:]:
                top = jnp.maximum(top, s)
            top = jnp.max(top, axis=1, keepdims=True)
            sums = None
            acc = None
            for j, s in enumerate(scores):
                p = jnp.exp(s - top)
                sums = p if sums is None else sums + p
                if j < PICKS:
                    slot, at = keys_at[j]
                    v = buf[slot, at, HD:]
                else:
                    v = g_kv[:, HD:]
                term = jnp.dot(p.astype(BF16), v, preferred_element_type=F32)
                acc = term if acc is None else acc + term
            context = acc / jnp.sum(sums, axis=1, keepdims=True)
            outs[side][span, :] = jnp.where(
                is_global[span], placed[span], context
            ).astype(BF16)


def attention(slots, rows, reach, queries, gslot, selected, pieces):
    return pl.pallas_call(
        attention_kernel,
        out_shape=(jax.ShapeDtypeStruct((ROWS, HD), BF16),) * 2,
        grid_spec=pltpu.PrefetchScalarGridSpec(
            num_scalar_prefetch=3,
            grid=(),
            in_specs=[vmem()] * 5
            + [pl.BlockSpec(memory_space=pl.ANY)] * len(pieces),
            out_specs=(vmem(),) * 2,
            scratch_shapes=[
                pltpu.VMEM((N_SEQ, UNIT, 2 * HD), BF16),
                pltpu.SemaphoreType.DMA((len(pieces),)),
            ],
        ),
        compiler_params=pltpu.CompilerParams(vmem_limit_bytes=48 << 20),
        cost_estimate=pl.CostEstimate(
            flops=2 << 30, transcendentals=3 << 20, bytes_accessed=8 << 20
        ),
        name="attention",
    )(slots, rows, reach, *queries, gslot, *selected, *[in_hbm(p) for p in pieces])


def on_device(
    activations, w_query, w_key, w_value, w_out, windows, rand_blocks, global_pos
):
    me = lax.axis_index("heads")
    here = lax.axis_index("seq")
    items = head_order()
    shifts = jnp.array([d for d, _ in items], jnp.int32)
    flips = jnp.array([e for _, e in items], jnp.int32)
    ids = (me // 2 + shifts + 8) % 8 * 2 + (me % 2 + flips) % 2

    def slot_of(seq):
        dx = (seq // 8 + here // 8) % 2
        dy = (seq // 2 % 4 - here // 2 % 4 + 4) % 4
        return dx * 8 + dy * 2 + (seq + here) % 2

    swap = lambda a: lax.ppermute(a, "seq", CORE)
    other = here + 1 - 2 * (here % 2)
    sides = jnp.stack([here, other])
    blocks = (
        sides[:, None] * BLK_DEV + jnp.arange(BLK_DEV, dtype=jnp.int32)[None, :]
    ).reshape(-1, 1)
    offsets = jnp.arange(SPAN, dtype=jnp.int32)[None, :] - WMAX
    near = (blocks + offsets + NBLK) % NBLK
    picks = jnp.concatenate([rand_blocks, swap(rand_blocks)], axis=0)
    named = jnp.concatenate([near, picks], axis=1).reshape(-1)
    key_slots = slot_of(named // BLK_DEV)
    key_rows = named % BLK_DEV * BLK

    owners = global_pos // ROWS
    order = jnp.arange(G, dtype=jnp.int32)
    earlier = (owners[:, None] == owners[None, :]) & (order[None, :] < order[:, None])
    ranks = jnp.sum(earlier.astype(jnp.int32), axis=1)
    gslot = (slot_of(owners) * GMAX + ranks)[:, None]
    local = owners[None, None, :] == sides[:, None, None]
    mine = local & (
        ranks[None, :] == jnp.arange(GMAX, dtype=jnp.int32)[:, None]
    )
    selected = jnp.max(jnp.where(mine, global_pos % ROWS, -1), axis=2)

    weights = (w_query, w_key, w_value)
    core = (here % 2)[None]
    odd = (here // 2 % 2)[None]

    class Projection:
        state = None

        def __call__(self, t, arrivals):
            acc = self.state and self.state[0]
            acc = project(ids, core, max(3 * t - 2, 0), arrivals, weights, acc)
            if t == 1:
                return acc, split_columns(core * 2 + odd, w_out)
            return (acc, *self.state[1:]) if self.state else (acc,)

    projection = Projection()
    last = gather_heads(activations, projection)
    acc, w_blocks = projection.state
    query, query_away, kv, kv_away = project(
        ids, core, 13, last, weights, acc, selected=selected[0][:, None]
    )
    query_here, w_blocks = lax.optimization_barrier((swap(query_away), w_blocks))
    w_quarter = lax.all_to_all(w_blocks, "heads", 0, 0)
    pieces = gather_seq(kv, swap(kv_away))
    context, context_away = attention(
        key_slots,
        key_rows,
        jnp.where(core > 0, windows[1:], windows[:1]),
        (query, query_here),
        gslot,
        (selected[:1], selected[1:]),
        pieces,
    )
    context = jnp.concatenate([context, swap(context_away)], axis=1)
    context, w_quarter = lax.optimization_barrier((context, w_quarter))
    w_half = (w_quarter, lax.ppermute(w_quarter, "seq", Y_PAIR))
    w_parts = (*w_half, *(swap(w) for w in w_half))

    class Combination:
        state = None
        waiting = ()

        def __call__(self, t, arrivals):
            self.waiting = (*self.waiting, *arrivals)
            if t < 2:
                return self.state
            start = 3 * t + 1 - len(self.waiting)
            out = combine(
                ids, odd, start, self.waiting, w_parts, self.state, last=t == 5
            )
            self.waiting = ()
            return out

    combination = Combination()
    return combination(5, gather_heads(context, combination))


def solution(mesh):
    in_specs = (
        P("seq", "heads"),
        P(None, "heads"),
        P(None, "heads"),
        P(None, "heads"),
        P("heads", None),
        P("heads"),
        P("seq", None),
        P(),
    )
    out_specs = P("seq", "heads")
    return jax.shard_map(
        on_device, mesh=mesh, in_specs=in_specs, out_specs=out_specs, check_vma=False
    )
```

```python
import math

import jax
import jax.numpy as jnp
from jax import lax
from jax.experimental import pallas as pl
from jax.experimental.pallas import tpu as pltpu
from jax.sharding import PartitionSpec as P

WMAX = 2
SPAN = 2 * WMAX + 1
R = 3
PICKS = SPAN + R
BLK = 128
BLK_DEV = 6
ROWS = BLK * BLK_DEV
GMAX = 32
G = 128
HD = 128
HEADS_DEV = 2
WIDTH = HD * HEADS_DEV
N_SEQ = 16
N_HEADS = 16
NBLK = N_SEQ * BLK_DEV
UNIT = ROWS + GMAX
NEGATIVE = -1e30
SCALE = 1.0 / math.sqrt(HD)
F32 = jnp.float32
BF16 = jnp.bfloat16

HEAD_SLOTS = (
    ((0, 0), (0, 0), (0, 0)),
    ((-1, 0), (1, 0), (-1, 0)),
    ((-2, 0), (2, 0), (1, 0)),
    ((-3, 0), (1, 1), (-2, 0)),
    ((-2, 1), (2, 1), (-4, 0)),
)
Z_UP = [(h, (h + 2) % 16) for h in range(16)]
Z_DOWN = [(h, (h - 2) % 16) for h in range(16)]
PAIR = [(h, h ^ 1) for h in range(16)]


def head_order():
    items = [(0, 0)]
    for up, down, across in HEAD_SLOTS:
        items += [
            (up[0] - 1, up[1]),
            (down[0] + 1, down[1]),
            (across[0], across[1] ^ 1),
        ]
    return items


Y_UP = [(s, (s // 8) * 8 + (s % 8 + 2) % 8) for s in range(16)]
Y_DOWN = [(s, (s // 8) * 8 + (s % 8 - 2) % 8) for s in range(16)]
HALF = [(s, s ^ 8) for s in range(16)]
CORE = [(s, s ^ 1) for s in range(16)]
Y_PAIR = [(s, s ^ 2) for s in range(16)]


def vmem():
    return pl.BlockSpec(memory_space=pltpu.VMEM)


def in_hbm(array):
    return pltpu.with_memory_space_constraint(array, pltpu.HBM)


def project_kernel(count, first, last, ids, core, *refs):
    xs, refs = refs[:count], refs[count:]
    ws, refs = refs[: 3 * count], refs[3 * count :]
    if not first:
        acc, refs = refs[0], refs[1:]
    if last:
        sel_ref, *outs = refs
    else:
        (out,) = refs
    parts = []
    for j in range(3):
        total = None if first else acc[:, j * WIDTH : (j + 1) * WIDTH]
        for i in range(count):
            term = jnp.dot(
                xs[i][...], ws[3 * i + j][...], preferred_element_type=F32
            )
            total = term if total is None else total + term
        if last:
            parts.append(total.astype(BF16))
        else:
            out[:, j * WIDTH : (j + 1) * WIDTH] = total
    if last:
        columns = lax.broadcasted_iota(jnp.int32, (GMAX, ROWS), 1)
        pick = jnp.where(columns == sel_ref[...], 1.0, 0.0).astype(BF16)
        second = core[0] > 0
        for j, part in enumerate(parts):
            chosen = jnp.dot(pick, part, preferred_element_type=F32).astype(BF16)
            low = max(j - 1, 0) * HD
            for rows, have in ((slice(0, ROWS), part), (slice(ROWS, UNIT), chosen)):
                left, right = have[:, :HD], have[:, HD:]
                q_or_kv = outs[:2] if j == 0 else outs[2:]
                q_or_kv[0][rows, low : low + HD] = jnp.where(second, right, left)
                q_or_kv[1][rows, low : low + HD] = jnp.where(second, left, right)


def project(ids, core, offset, xs, weights, acc, selected=None):
    count = len(xs)
    first, last = acc is None, selected is not None
    full = lambda shape: pl.BlockSpec(shape, lambda g, ids, core: (0, 0))
    in_specs = [full((ROWS, WIDTH)) for _ in xs]
    operands = list(xs)
    for i in range(count):
        for w in weights:
            in_specs.append(
                pl.BlockSpec((WIDTH, WIDTH), lambda g, ids, core, i=i: (ids[offset + i], 0))
            )
            operands.append(in_hbm(w))
    aliases = {}
    if not first:
        in_specs.append(full((ROWS, 3 * WIDTH)))
        operands.append(acc)
        if not last:
            aliases = {len(operands) + 1: 0}
    if last:
        in_specs.append(full((GMAX, 1)))
        operands.append(selected)
        shapes = ((UNIT, HD),) * 2 + ((UNIT, 2 * HD),) * 2
        out_shape = tuple(jax.ShapeDtypeStruct(shape, BF16) for shape in shapes)
        out_specs = tuple(full(shape) for shape in shapes)
    else:
        out_shape = jax.ShapeDtypeStruct((ROWS, 3 * WIDTH), F32)
        out_specs = full((ROWS, 3 * WIDTH))

    def body(*refs):
        project_kernel(count, first, last, *refs)

    return pl.pallas_call(
        body,
        out_shape=out_shape,
        grid_spec=pltpu.PrefetchScalarGridSpec(
            num_scalar_prefetch=2, grid=(1,), in_specs=in_specs, out_specs=out_specs
        ),
        input_output_aliases=aliases,
        compiler_params=pltpu.CompilerParams(vmem_limit_bytes=40 << 20),
        cost_estimate=pl.CostEstimate(
            flops=2 * count * ROWS * WIDTH * 3 * WIDTH,
            transcendentals=0,
            bytes_accessed=6 << 20,
        ),
        name="project",
    )(ids, core, *operands)


def combine_kernel(count, first, last, ids, odd, *refs):
    cs, refs = refs[:count], refs[count:]
    ws, refs = refs[: 4 * count], refs[4 * count :]
    flip = odd[0] > 0
    total = None
    if not first:
        acc, refs = refs[0], refs[1:]
        total = acc[...]
    (out,) = refs
    for i in range(count):
        quarters = [w[0] for w in ws[4 * i : 4 * i + 4]]
        w = jnp.concatenate(
            [
                jnp.where(flip, quarters[n ^ 1], quarters[n])
                for n in range(4)
            ],
            axis=0,
        )
        part = jnp.dot(cs[i][...], w, preferred_element_type=F32)
        part = part.astype(BF16).astype(F32)
        total = part if total is None else total + part
    out[...] = total.astype(out.dtype)


def combine(ids, odd, offset, cs, w_parts, acc, last=False):
    count = len(cs)
    first = acc is None
    full = lambda shape: pl.BlockSpec(shape, lambda g, ids, odd: (0, 0))
    in_specs = [full((ROWS, WIDTH)) for _ in cs]
    operands = list(cs)
    for i in range(count):
        for w in w_parts:
            in_specs.append(
                pl.BlockSpec(
                    (1, WIDTH // 4, WIDTH),
                    lambda g, ids, odd, i=i: (ids[offset + i], 0, 0),
                )
            )
            operands.append(in_hbm(w))
    aliases = {}
    if not first:
        in_specs.append(full((ROWS, WIDTH)))
        operands.append(acc)
        if not last:
            aliases = {len(operands) + 1: 0}

    def body(*refs):
        combine_kernel(count, first, last, *refs)

    return pl.pallas_call(
        body,
        out_shape=jax.ShapeDtypeStruct((ROWS, WIDTH), BF16 if last else F32),
        grid_spec=pltpu.PrefetchScalarGridSpec(
            num_scalar_prefetch=2,
            grid=(1,),
            in_specs=in_specs,
            out_specs=full((ROWS, WIDTH)),
        ),
        input_output_aliases=aliases,
        compiler_params=pltpu.CompilerParams(vmem_limit_bytes=40 << 20),
        cost_estimate=pl.CostEstimate(
            flops=2 * count * ROWS * WIDTH * WIDTH,
            transcendentals=0,
            bytes_accessed=3 << 20,
        ),
        name="combine",
    )(ids, odd, *operands)


def split_kernel(quarter, w_ref, out_ref):
    for j in range(N_HEADS):
        out_ref[j] = w_ref[:, j * WIDTH : (j + 1) * WIDTH]


def split_columns(quarter, w_out):
    rows = WIDTH // 4
    return pl.pallas_call(
        split_kernel,
        out_shape=jax.ShapeDtypeStruct((N_HEADS, rows, WIDTH), BF16),
        grid_spec=pltpu.PrefetchScalarGridSpec(
            num_scalar_prefetch=1,
            grid=(1,),
            in_specs=[
                pl.BlockSpec(
                    (rows, N_HEADS * WIDTH), lambda g, quarter: (quarter[0], 0)
                )
            ],
            out_specs=pl.BlockSpec(
                (N_HEADS, rows, WIDTH), lambda g, quarter: (0, 0, 0)
            ),
        ),
        cost_estimate=pl.CostEstimate(
            flops=0, transcendentals=0, bytes_accessed=1 << 20
        ),
        name="split_columns",
    )(quarter, in_hbm(w_out))


def gather_heads(own, work):
    have = {(0, 0): own}
    before = [own]
    state = None
    for t, (up, down, across) in enumerate(HEAD_SLOTS):
        ready = [have[up], have[down], have[across]]
        if state is not None:
            ready = [lax.optimization_barrier((item, state))[0] for item in ready]
        got = [
            lax.ppermute(ready[0], "heads", Z_UP),
            lax.ppermute(ready[1], "heads", Z_DOWN),
            lax.ppermute(ready[2], "heads", PAIR),
        ]
        state = work.state = work(t, before)
        have[(up[0] - 1, up[1])] = got[0]
        have[(down[0] + 1, down[1])] = got[1]
        have[(across[0], across[1] ^ 1)] = got[2]
        before = got
    return before


def gather_seq(mine, theirs):
    up = lambda a: lax.ppermute(a, "seq", Y_UP)
    down = lambda a: lax.ppermute(a, "seq", Y_DOWN)
    half = lambda a: lax.ppermute(a, "seq", HALF)
    near = ({(0, 0): mine}, {(0, 0): theirs})
    for n in near:
        n[1, 0] = half(n[0, 0])
        n[0, 3] = up(n[0, 0])
        n[0, 1] = down(n[0, 0])
    for n in near:
        n[1, 3] = half(n[0, 3])
        n[0, 2] = up(n[0, 3])
        n[1, 1] = down(n[1, 0])
    near[0][1, 2] = up(near[0][1, 3])
    near[1][1, 2] = down(near[1][1, 1])
    return [near[slot % 2][slot // 8, slot // 2 % 4] for slot in range(N_SEQ)]


def attention_kernel(slots, rows, reach, *refs):
    queries, (gslot_ref, *sels), refs = refs[:2], refs[2:5], refs[5:]
    pieces, (*outs, buf, sems) = refs[:N_SEQ], refs[N_SEQ:]
    copies = [
        pltpu.make_async_copy(pieces[i], buf.at[i], sems.at[i]) for i in range(N_SEQ)
    ]
    for copy in copies:
        copy.start()
    for copy in copies:
        copy.wait()

    dims = (((1,), (1,)), ((), ()))

    def scored(q, k):
        return lax.dot_general(q, k, dims, preferred_element_type=F32) * SCALE

    found = jnp.concatenate([buf[i, ROWS:UNIT, :] for i in range(N_SEQ)], axis=0)
    where = lax.broadcasted_iota(jnp.int32, (G, N_SEQ * GMAX), 1)
    pick = jnp.where(where == gslot_ref[...], 1.0, 0.0).astype(BF16)
    g_kv = jnp.dot(pick, found, preferred_element_type=F32).astype(BF16)

    g_query = jnp.concatenate([q[ROWS:UNIT, :] for q in queries], axis=0)
    g_scores = [scored(g_query, buf[i, :ROWS, :HD]) for i in range(N_SEQ)]
    top = g_scores[0]
    for s in g_scores[1:]:
        top = jnp.maximum(top, s)
    top = jnp.max(top, axis=1, keepdims=True)
    sums = jnp.zeros((2 * GMAX, ROWS), F32)
    acc = jnp.zeros((2 * GMAX, HD), F32)
    for i in range(N_SEQ):
        p = jnp.exp(g_scores[i] - top)
        sums = sums + p
        acc = acc + jnp.dot(
            p.astype(BF16), buf[i, :ROWS, HD:], preferred_element_type=F32
        )
    g_context = (acc / jnp.sum(sums, axis=1, keepdims=True)).astype(BF16)

    wide = reach[0] >= WMAX
    for side in range(2):
        steps = lax.broadcasted_iota(jnp.int32, (ROWS, GMAX), 0)
        place = jnp.where(steps == sels[side][...], 1.0, 0.0)
        is_global = jnp.sum(place, axis=1, keepdims=True) > 0.5
        placed = jnp.dot(
            place.astype(BF16),
            g_context[side * GMAX : (side + 1) * GMAX],
            preferred_element_type=F32,
        )
        for b in range(BLK_DEV):
            span = slice(b * BLK, (b + 1) * BLK)
            query = queries[side][span, :]
            first = (side * BLK_DEV + b) * PICKS
            keys_at = [
                (slots[first + j], pl.ds(pl.multiple_of(rows[first + j], BLK), BLK))
                for j in range(PICKS)
            ]
            scores = [scored(query, buf[slot, at, :HD]) for slot, at in keys_at]
            for j in (0, SPAN - 1):
                scores[j] = jnp.where(wide, scores[j], NEGATIVE)
            scores.append(scored(query, g_kv[:, :HD]))
            top = scores[0]
            for s in scores[1:]:
                top = jnp.maximum(top, s)
            top = jnp.max(top, axis=1, keepdims=True)
            sums = None
            acc = None
            for j, s in enumerate(scores):
                p = jnp.exp(s - top)
                sums = p if sums is None else sums + p
                if j < PICKS:
                    slot, at = keys_at[j]
                    v = buf[slot, at, HD:]
                else:
                    v = g_kv[:, HD:]
                term = jnp.dot(p.astype(BF16), v, preferred_element_type=F32)
                acc = term if acc is None else acc + term
            context = acc / jnp.sum(sums, axis=1, keepdims=True)
            outs[side][span, :] = jnp.where(
                is_global[span], placed[span], context
            ).astype(BF16)


def attention(slots, rows, reach, queries, gslot, selected, pieces):
    return pl.pallas_call(
        attention_kernel,
        out_shape=(jax.ShapeDtypeStruct((ROWS, HD), BF16),) * 2,
        grid_spec=pltpu.PrefetchScalarGridSpec(
            num_scalar_prefetch=3,
            grid=(),
            in_specs=[vmem()] * 5
            + [pl.BlockSpec(memory_space=pl.ANY)] * len(pieces),
            out_specs=(vmem(),) * 2,
            scratch_shapes=[
                pltpu.VMEM((N_SEQ, UNIT, 2 * HD), BF16),
                pltpu.SemaphoreType.DMA((len(pieces),)),
            ],
        ),
        compiler_params=pltpu.CompilerParams(vmem_limit_bytes=48 << 20),
        cost_estimate=pl.CostEstimate(
            flops=2 << 30, transcendentals=3 << 20, bytes_accessed=8 << 20
        ),
        name="attention",
    )(slots, rows, reach, *queries, gslot, *selected, *[in_hbm(p) for p in pieces])


def on_device(
    activations, w_query, w_key, w_value, w_out, windows, rand_blocks, global_pos
):
    me = lax.axis_index("heads")
    here = lax.axis_index("seq")
    items = head_order()
    shifts = jnp.array([d for d, _ in items], jnp.int32)
    flips = jnp.array([e for _, e in items], jnp.int32)
    ids = (me // 2 + shifts + 8) % 8 * 2 + (me % 2 + flips) % 2

    def slot_of(seq):
        dx = (seq // 8 + here // 8) % 2
        dy = (seq // 2 % 4 - here // 2 % 4 + 4) % 4
        return dx * 8 + dy * 2 + (seq + here) % 2

    swap = lambda a: lax.ppermute(a, "seq", CORE)
    other = here + 1 - 2 * (here % 2)
    sides = jnp.stack([here, other])
    blocks = (
        sides[:, None] * BLK_DEV + jnp.arange(BLK_DEV, dtype=jnp.int32)[None, :]
    ).reshape(-1, 1)
    offsets = jnp.arange(SPAN, dtype=jnp.int32)[None, :] - WMAX
    near = (blocks + offsets + NBLK) % NBLK
    picks = jnp.concatenate([rand_blocks, swap(rand_blocks)], axis=0)
    named = jnp.concatenate([near, picks], axis=1).reshape(-1)
    key_slots = slot_of(named // BLK_DEV)
    key_rows = named % BLK_DEV * BLK

    owners = global_pos // ROWS
    order = jnp.arange(G, dtype=jnp.int32)
    earlier = (owners[:, None] == owners[None, :]) & (order[None, :] < order[:, None])
    ranks = jnp.sum(earlier.astype(jnp.int32), axis=1)
    gslot = (slot_of(owners) * GMAX + ranks)[:, None]
    local = owners[None, None, :] == sides[:, None, None]
    mine = local & (
        ranks[None, :] == jnp.arange(GMAX, dtype=jnp.int32)[:, None]
    )
    selected = jnp.max(jnp.where(mine, global_pos % ROWS, -1), axis=2)

    weights = (w_query, w_key, w_value)
    core = (here % 2)[None]
    odd = (here // 2 % 2)[None]

    class Projection:
        state = None

        def __call__(self, t, arrivals):
            acc = self.state and self.state[0]
            acc = project(ids, core, max(3 * t - 2, 0), arrivals, weights, acc)
            if t == 1:
                return acc, split_columns(core * 2 + odd, w_out)
            return (acc, *self.state[1:]) if self.state else (acc,)

    projection = Projection()
    last = gather_heads(activations, projection)
    acc, w_blocks = projection.state
    query, query_away, kv, kv_away = project(
        ids, core, 13, last, weights, acc, selected=selected[0][:, None]
    )
    query_here, w_blocks = lax.optimization_barrier((swap(query_away), w_blocks))
    w_quarter = lax.all_to_all(w_blocks, "heads", 0, 0)
    pieces = gather_seq(kv, swap(kv_away))
    context, context_away = attention(
        key_slots,
        key_rows,
        jnp.where(core > 0, windows[1:], windows[:1]),
        (query, query_here),
        gslot,
        (selected[:1], selected[1:]),
        pieces,
    )
    context = jnp.concatenate([context, swap(context_away)], axis=1)
    context, w_quarter = lax.optimization_barrier((context, w_quarter))
    w_half = (w_quarter, lax.ppermute(w_quarter, "seq", Y_PAIR))
    w_parts = (*w_half, *(swap(w) for w in w_half))

    class Combination:
        state = None
        waiting = ()

        def __call__(self, t, arrivals):
            self.waiting = (*self.waiting, *arrivals)
            if t < 2:
                return self.state
            start = 3 * t + 1 - len(self.waiting)
            out = combine(
                ids, odd, start, self.waiting, w_parts, self.state, last=t == 5
            )
            self.waiting = ()
            return out

    combination = Combination()
    return combination(5, gather_heads(context, combination))


def solution(mesh):
    in_specs = (
        P("seq", "heads"),
        P(None, "heads"),
        P(None, "heads"),
        P(None, "heads"),
        P("heads", None),
        P("heads"),
        P("seq", None),
        P(),
    )
    out_specs = P("seq", "heads")
    return jax.shard_map(
        on_device, mesh=mesh, in_specs=in_specs, out_specs=out_specs, check_vma=False
    )
```

```python
import math

import jax
import jax.numpy as jnp
from jax import lax
from jax.experimental import pallas as pl
from jax.experimental.pallas import tpu as pltpu
from jax.sharding import PartitionSpec as P

WMAX = 2
SPAN = 2 * WMAX + 1
R = 3
PICKS = SPAN + R
BLK = 128
BLK_DEV = 6
ROWS = BLK * BLK_DEV
GMAX = 32
G = 128
HD = 128
HEADS_DEV = 2
WIDTH = HD * HEADS_DEV
N_SEQ = 16
N_HEADS = 16
NBLK = N_SEQ * BLK_DEV
UNIT = ROWS + GMAX
NEGATIVE = -1e30
SCALE = 1.0 / math.sqrt(HD)
F32 = jnp.float32
BF16 = jnp.bfloat16

HEAD_SLOTS = (
    ((0, 0), (0, 0), (0, 0)),
    ((-1, 0), (1, 0), (-1, 0)),
    ((-2, 0), (2, 0), (1, 0)),
    ((-3, 0), (1, 1), (-2, 0)),
    ((-2, 1), (2, 1), (-4, 0)),
)
Z_UP = [(h, (h + 2) % 16) for h in range(16)]
Z_DOWN = [(h, (h - 2) % 16) for h in range(16)]
PAIR = [(h, h ^ 1) for h in range(16)]


def head_order():
    items = [(0, 0)]
    for up, down, across in HEAD_SLOTS:
        items += [
            (up[0] - 1, up[1]),
            (down[0] + 1, down[1]),
            (across[0], across[1] ^ 1),
        ]
    return items


Y_UP = [(s, (s // 8) * 8 + (s % 8 + 2) % 8) for s in range(16)]
Y_DOWN = [(s, (s // 8) * 8 + (s % 8 - 2) % 8) for s in range(16)]
HALF = [(s, s ^ 8) for s in range(16)]
CORE = [(s, s ^ 1) for s in range(16)]
Y_PAIR = [(s, s ^ 2) for s in range(16)]


def vmem():
    return pl.BlockSpec(memory_space=pltpu.VMEM)


def in_hbm(array):
    return pltpu.with_memory_space_constraint(array, pltpu.HBM)


def project_kernel(count, n_w, first, last, ids, core, *refs):
    xs, refs = refs[:count], refs[count:]
    ws, refs = refs[: n_w * count], refs[n_w * count :]
    if not first:
        acc, refs = refs[0], refs[1:]
    if last:
        sel_ref, ours, theirs = refs
    else:
        (out,) = refs
    parts = []
    for j in range(n_w):
        total = None if first else acc[:, j * WIDTH : (j + 1) * WIDTH]
        for i in range(count):
            term = jnp.dot(xs[i][...], ws[n_w * i + j][...], preferred_element_type=F32)
            total = term if total is None else total + term
        if last:
            parts.append(total.astype(BF16))
        else:
            out[:, j * WIDTH : (j + 1) * WIDTH] = total
    if last:
        columns = lax.broadcasted_iota(jnp.int32, (GMAX, ROWS), 1)
        pick = jnp.where(columns == sel_ref[...], 1.0, 0.0).astype(BF16)
        second = core[0] > 0
        for j, part in enumerate(parts):
            chosen = jnp.dot(pick, part, preferred_element_type=F32).astype(BF16)
            span = slice(j * HD, (j + 1) * HD)
            for rows, have in ((slice(0, ROWS), part), (slice(ROWS, UNIT), chosen)):
                left, right = have[:, :HD], have[:, HD:]
                ours[rows, span] = jnp.where(second, right, left)
                theirs[rows, span] = jnp.where(second, left, right)


def project(ids, core, offset, xs, weights, acc, selected=None):
    count, n_w = len(xs), len(weights)
    first, last = acc is None, selected is not None
    full = lambda shape: pl.BlockSpec(shape, lambda g, ids, core: (0, 0))
    in_specs = [full((ROWS, WIDTH)) for _ in xs]
    operands = list(xs)
    for i in range(count):
        for w in weights:
            in_specs.append(
                pl.BlockSpec(
                    (WIDTH, WIDTH), lambda g, ids, core, i=i: (ids[offset + i], 0)
                )
            )
            operands.append(in_hbm(w))
    aliases = {}
    if not first:
        in_specs.append(full((ROWS, n_w * WIDTH)))
        operands.append(acc)
        if not last:
            aliases = {len(operands) + 1: 0}
    if last:
        in_specs.append(full((GMAX, 1)))
        operands.append(selected)
        out_shape = (jax.ShapeDtypeStruct((UNIT, n_w * HD), BF16),) * 2
        out_specs = (full((UNIT, n_w * HD)),) * 2
    else:
        out_shape = jax.ShapeDtypeStruct((ROWS, n_w * WIDTH), F32)
        out_specs = full((ROWS, n_w * WIDTH))

    def body(*refs):
        project_kernel(count, n_w, first, last, *refs)

    return pl.pallas_call(
        body,
        out_shape=out_shape,
        grid_spec=pltpu.PrefetchScalarGridSpec(
            num_scalar_prefetch=2, grid=(1,), in_specs=in_specs, out_specs=out_specs
        ),
        input_output_aliases=aliases,
        compiler_params=pltpu.CompilerParams(vmem_limit_bytes=40 << 20),
        cost_estimate=pl.CostEstimate(
            flops=2 * count * ROWS * WIDTH * n_w * WIDTH,
            transcendentals=0,
            bytes_accessed=6 << 20,
        ),
        name="project",
    )(ids, core, *operands)


def combine_kernel(count, first, last, ids, odd, *refs):
    cs, refs = refs[:count], refs[count:]
    ws, refs = refs[: 4 * count], refs[4 * count :]
    flip = odd[0] > 0
    total = None
    if not first:
        acc, refs = refs[0], refs[1:]
        total = acc[...]
    (out,) = refs
    for i in range(count):
        quarters = [w[0] for w in ws[4 * i : 4 * i + 4]]
        w = jnp.concatenate(
            [
                jnp.where(flip, quarters[n ^ 1], quarters[n])
                for n in range(4)
            ],
            axis=0,
        )
        part = jnp.dot(cs[i][...], w, preferred_element_type=F32)
        part = part.astype(BF16).astype(F32)
        total = part if total is None else total + part
    out[...] = total.astype(out.dtype)


def combine(ids, odd, offset, cs, w_parts, acc, last=False):
    count = len(cs)
    first = acc is None
    full = lambda shape: pl.BlockSpec(shape, lambda g, ids, odd: (0, 0))
    in_specs = [full((ROWS, WIDTH)) for _ in cs]
    operands = list(cs)
    for i in range(count):
        for w in w_parts:
            in_specs.append(
                pl.BlockSpec(
                    (1, WIDTH // 4, WIDTH),
                    lambda g, ids, odd, i=i: (ids[offset + i], 0, 0),
                )
            )
            operands.append(in_hbm(w))
    aliases = {}
    if not first:
        in_specs.append(full((ROWS, WIDTH)))
        operands.append(acc)
        if not last:
            aliases = {len(operands) + 1: 0}

    def body(*refs):
        combine_kernel(count, first, last, *refs)

    return pl.pallas_call(
        body,
        out_shape=jax.ShapeDtypeStruct((ROWS, WIDTH), BF16 if last else F32),
        grid_spec=pltpu.PrefetchScalarGridSpec(
            num_scalar_prefetch=2,
            grid=(1,),
            in_specs=in_specs,
            out_specs=full((ROWS, WIDTH)),
        ),
        input_output_aliases=aliases,
        compiler_params=pltpu.CompilerParams(vmem_limit_bytes=40 << 20),
        cost_estimate=pl.CostEstimate(
            flops=2 * count * ROWS * WIDTH * WIDTH,
            transcendentals=0,
            bytes_accessed=3 << 20,
        ),
        name="combine",
    )(ids, odd, *operands)


def split_kernel(quarter, w_ref, out_ref):
    for j in range(N_HEADS):
        out_ref[j] = w_ref[:, j * WIDTH : (j + 1) * WIDTH]


def split_columns(quarter, w_out):
    rows = WIDTH // 4
    return pl.pallas_call(
        split_kernel,
        out_shape=jax.ShapeDtypeStruct((N_HEADS, rows, WIDTH), BF16),
        grid_spec=pltpu.PrefetchScalarGridSpec(
            num_scalar_prefetch=1,
            grid=(1,),
            in_specs=[
                pl.BlockSpec(
                    (rows, N_HEADS * WIDTH), lambda g, quarter: (quarter[0], 0)
                )
            ],
            out_specs=pl.BlockSpec(
                (N_HEADS, rows, WIDTH), lambda g, quarter: (0, 0, 0)
            ),
        ),
        cost_estimate=pl.CostEstimate(
            flops=0, transcendentals=0, bytes_accessed=1 << 20
        ),
        name="split_columns",
    )(quarter, in_hbm(w_out))


def gather_heads(own, work):
    have = {(0, 0): own}
    before = [own]
    state = None
    for t, (up, down, across) in enumerate(HEAD_SLOTS):
        ready = [have[up], have[down], have[across]]
        if state is not None:
            ready = [lax.optimization_barrier((item, state))[0] for item in ready]
        got = [
            lax.ppermute(ready[0], "heads", Z_UP),
            lax.ppermute(ready[1], "heads", Z_DOWN),
            lax.ppermute(ready[2], "heads", PAIR),
        ]
        state = work.state = work(t, before)
        have[(up[0] - 1, up[1])] = got[0]
        have[(down[0] + 1, down[1])] = got[1]
        have[(across[0], across[1] ^ 1)] = got[2]
        before = got
    return before


def gather_seq(mine, theirs):
    up = lambda a: lax.ppermute(a, "seq", Y_UP)
    down = lambda a: lax.ppermute(a, "seq", Y_DOWN)
    half = lambda a: lax.ppermute(a, "seq", HALF)
    near = ({(0, 0): mine}, {(0, 0): theirs})
    for n in near:
        n[1, 0] = half(n[0, 0])
        n[0, 3] = up(n[0, 0])
        n[0, 1] = down(n[0, 0])
    for n in near:
        n[1, 3] = half(n[0, 3])
        n[0, 2] = up(n[0, 3])
        n[1, 1] = down(n[1, 0])
    near[0][1, 2] = up(near[0][1, 3])
    near[1][1, 2] = down(near[1][1, 1])
    return [near[slot % 2][slot // 8, slot // 2 % 4] for slot in range(N_SEQ)]


def attention_kernel(slots, rows, reach, *refs):
    queries, (gslot_ref, *sels), refs = refs[:2], refs[2:5], refs[5:]
    pieces, (*outs, buf, sems) = refs[:N_SEQ], refs[N_SEQ:]
    copies = [
        pltpu.make_async_copy(pieces[i], buf.at[i], sems.at[i]) for i in range(N_SEQ)
    ]
    for copy in copies:
        copy.start()
    for copy in copies:
        copy.wait()

    dims = (((1,), (1,)), ((), ()))

    def scored(q, k):
        return lax.dot_general(q, k, dims, preferred_element_type=F32) * SCALE

    found = jnp.concatenate([buf[i, ROWS:UNIT, :] for i in range(N_SEQ)], axis=0)
    where = lax.broadcasted_iota(jnp.int32, (G, N_SEQ * GMAX), 1)
    pick = jnp.where(where == gslot_ref[...], 1.0, 0.0).astype(BF16)
    g_kv = jnp.dot(pick, found, preferred_element_type=F32).astype(BF16)

    g_query = jnp.concatenate([q[ROWS:UNIT, :] for q in queries], axis=0)
    g_scores = [scored(g_query, buf[i, :ROWS, :HD]) for i in range(N_SEQ)]
    top = g_scores[0]
    for s in g_scores[1:]:
        top = jnp.maximum(top, s)
    top = jnp.max(top, axis=1, keepdims=True)
    sums = jnp.zeros((2 * GMAX, ROWS), F32)
    acc = jnp.zeros((2 * GMAX, HD), F32)
    for i in range(N_SEQ):
        p = jnp.exp(g_scores[i] - top)
        sums = sums + p
        acc = acc + jnp.dot(
            p.astype(BF16), buf[i, :ROWS, HD:], preferred_element_type=F32
        )
    g_context = (acc / jnp.sum(sums, axis=1, keepdims=True)).astype(BF16)

    wide = reach[0] >= WMAX
    for side in range(2):
        steps = lax.broadcasted_iota(jnp.int32, (ROWS, GMAX), 0)
        place = jnp.where(steps == sels[side][...], 1.0, 0.0)
        is_global = jnp.sum(place, axis=1, keepdims=True) > 0.5
        placed = jnp.dot(
            place.astype(BF16),
            g_context[side * GMAX : (side + 1) * GMAX],
            preferred_element_type=F32,
        )
        for b in range(BLK_DEV):
            span = slice(b * BLK, (b + 1) * BLK)
            query = queries[side][span, :]
            first = (side * BLK_DEV + b) * PICKS
            keys_at = [
                (slots[first + j], pl.ds(pl.multiple_of(rows[first + j], BLK), BLK))
                for j in range(PICKS)
            ]
            keys = [buf[slot, at, :HD] for slot, at in keys_at] + [g_kv[:, :HD]]
            values = [buf[slot, at, HD:] for slot, at in keys_at] + [g_kv[:, HD:]]
            scores = scored(query, jnp.concatenate(keys, axis=0))
            scores = [
                jnp.where(wide, scores[:, :BLK], NEGATIVE),
                scores[:, BLK : (SPAN - 1) * BLK],
                jnp.where(wide, scores[:, (SPAN - 1) * BLK : SPAN * BLK], NEGATIVE),
                scores[:, SPAN * BLK :],
            ]
            scores = jnp.concatenate(scores, axis=1)
            top = jnp.max(scores, axis=1, keepdims=True)
            p = jnp.exp(scores - top)
            acc = jnp.dot(
                p.astype(BF16),
                jnp.concatenate(values, axis=0),
                preferred_element_type=F32,
            )
            context = acc / jnp.sum(p, axis=1, keepdims=True)
            outs[side][span, :] = jnp.where(
                is_global[span], placed[span], context
            ).astype(BF16)


def attention(slots, rows, reach, queries, gslot, selected, pieces):
    return pl.pallas_call(
        attention_kernel,
        out_shape=(jax.ShapeDtypeStruct((ROWS, HD), BF16),) * 2,
        grid_spec=pltpu.PrefetchScalarGridSpec(
            num_scalar_prefetch=3,
            grid=(),
            in_specs=[vmem()] * 5
            + [pl.BlockSpec(memory_space=pl.ANY)] * len(pieces),
            out_specs=(vmem(),) * 2,
            scratch_shapes=[
                pltpu.VMEM((N_SEQ, UNIT, 2 * HD), BF16),
                pltpu.SemaphoreType.DMA((len(pieces),)),
            ],
        ),
        compiler_params=pltpu.CompilerParams(vmem_limit_bytes=48 << 20),
        cost_estimate=pl.CostEstimate(
            flops=2 << 30, transcendentals=3 << 20, bytes_accessed=8 << 20
        ),
        name="attention",
    )(slots, rows, reach, *queries, gslot, *selected, *[in_hbm(p) for p in pieces])


def on_device(
    activations, w_query, w_key, w_value, w_out, windows, rand_blocks, global_pos
):
    me = lax.axis_index("heads")
    here = lax.axis_index("seq")
    items = head_order()
    shifts = jnp.array([d for d, _ in items], jnp.int32)
    flips = jnp.array([e for _, e in items], jnp.int32)
    ids = (me // 2 + shifts + 8) % 8 * 2 + (me % 2 + flips) % 2

    def slot_of(seq):
        dx = (seq // 8 + here // 8) % 2
        dy = (seq // 2 % 4 - here // 2 % 4 + 4) % 4
        return dx * 8 + dy * 2 + (seq + here) % 2

    swap = lambda a: lax.ppermute(a, "seq", CORE)
    other = here + 1 - 2 * (here % 2)
    sides = jnp.stack([here, other])
    blocks = (
        sides[:, None] * BLK_DEV + jnp.arange(BLK_DEV, dtype=jnp.int32)[None, :]
    ).reshape(-1, 1)
    offsets = jnp.arange(SPAN, dtype=jnp.int32)[None, :] - WMAX
    near = (blocks + offsets + NBLK) % NBLK
    picks = jnp.concatenate([rand_blocks, swap(rand_blocks)], axis=0)
    named = jnp.concatenate([near, picks], axis=1).reshape(-1)
    key_slots = slot_of(named // BLK_DEV)
    key_rows = named % BLK_DEV * BLK

    owners = global_pos // ROWS
    order = jnp.arange(G, dtype=jnp.int32)
    earlier = (owners[:, None] == owners[None, :]) & (order[None, :] < order[:, None])
    ranks = jnp.sum(earlier.astype(jnp.int32), axis=1)
    gslot = (slot_of(owners) * GMAX + ranks)[:, None]
    local = owners[None, None, :] == sides[:, None, None]
    mine = local & (
        ranks[None, :] == jnp.arange(GMAX, dtype=jnp.int32)[:, None]
    )
    selected = jnp.max(jnp.where(mine, global_pos % ROWS, -1), axis=2)

    weights = (w_key, w_value)
    core = (here % 2)[None]
    odd = (here // 2 % 2)[None]

    shards = []

    class Projection:
        state = None

        def __call__(self, t, arrivals):
            shards.extend(arrivals)
            acc = self.state and self.state[0]
            acc = project(ids, core, max(3 * t - 2, 0), arrivals, weights, acc)
            if t == 1:
                return acc, split_columns(core * 2 + odd, w_out)
            return (acc, *self.state[1:]) if self.state else (acc,)

    projection = Projection()
    last = gather_heads(activations, projection)
    acc, w_blocks = projection.state
    kv, kv_away = project(
        ids, core, 13, last, weights, acc, selected=selected[0][:, None]
    )
    query, query_away = project(
        ids,
        core,
        0,
        [*shards, *last],
        (w_query,),
        None,
        selected=selected[0][:, None],
    )
    pieces = gather_seq(kv, swap(kv_away))
    query_here = swap(query_away)
    pieces[6], w_blocks = lax.optimization_barrier((pieces[6], w_blocks))
    w_quarter = lax.all_to_all(w_blocks, "heads", 0, 0)
    pieces, w_quarter = lax.optimization_barrier((pieces, w_quarter))
    w_half = (w_quarter, lax.ppermute(w_quarter, "seq", Y_PAIR))
    context, context_away = attention(
        key_slots,
        key_rows,
        jnp.where(core > 0, windows[1:], windows[:1]),
        (query, query_here),
        gslot,
        (selected[:1], selected[1:]),
        pieces,
    )
    context = jnp.concatenate([context, swap(context_away)], axis=1)
    context, w_half = lax.optimization_barrier((context, w_half))
    w_parts = (*w_half, *(swap(w) for w in w_half))

    class Combination:
        state = None
        waiting = ()

        def __call__(self, t, arrivals):
            self.waiting = (*self.waiting, *arrivals)
            if t < 2:
                return self.state
            start = 3 * t + 1 - len(self.waiting)
            out = combine(
                ids, odd, start, self.waiting, w_parts, self.state, last=t == 5
            )
            self.waiting = ()
            return out

    combination = Combination()
    return combination(5, gather_heads(context, combination))


def solution(mesh):
    in_specs = (
        P("seq", "heads"),
        P(None, "heads"),
        P(None, "heads"),
        P(None, "heads"),
        P("heads", None),
        P("heads"),
        P("seq", None),
        P(),
    )
    out_specs = P("seq", "heads")
    return jax.shard_map(
        on_device, mesh=mesh, in_specs=in_specs, out_specs=out_specs, check_vma=False
    )
```

```python
import math

import jax
import jax.numpy as jnp
from jax import lax
from jax.experimental import pallas as pl
from jax.experimental.pallas import tpu as pltpu
from jax.sharding import PartitionSpec as P

WMAX = 2
SPAN = 2 * WMAX + 1
R = 3
PICKS = SPAN + R
BLK = 128
BLK_DEV = 6
ROWS = BLK * BLK_DEV
GMAX = 32
G = 128
HD = 128
HEADS_DEV = 2
WIDTH = HD * HEADS_DEV
N_SEQ = 16
N_HEADS = 16
NBLK = N_SEQ * BLK_DEV
UNIT = ROWS + GMAX
NEGATIVE = -1e30
SCALE = 1.0 / math.sqrt(HD)
F32 = jnp.float32
BF16 = jnp.bfloat16

HEAD_SLOTS = (
    ((0, 0), (0, 0), (0, 0)),
    ((-1, 0), (1, 0), (-1, 0)),
    ((-2, 0), (2, 0), (1, 0)),
    ((-3, 0), (1, 1), (-2, 0)),
    ((-2, 1), (2, 1), (-4, 0)),
)
Z_UP = [(h, (h + 2) % 16) for h in range(16)]
Z_DOWN = [(h, (h - 2) % 16) for h in range(16)]
PAIR = [(h, h ^ 1) for h in range(16)]


def head_order():
    items = [(0, 0)]
    for up, down, across in HEAD_SLOTS:
        items += [
            (up[0] - 1, up[1]),
            (down[0] + 1, down[1]),
            (across[0], across[1] ^ 1),
        ]
    return items


Y_UP = [(s, (s // 8) * 8 + (s % 8 + 2) % 8) for s in range(16)]
Y_DOWN = [(s, (s // 8) * 8 + (s % 8 - 2) % 8) for s in range(16)]
HALF = [(s, s ^ 8) for s in range(16)]
CORE = [(s, s ^ 1) for s in range(16)]
Y_PAIR = [(s, s ^ 2) for s in range(16)]


def vmem():
    return pl.BlockSpec(memory_space=pltpu.VMEM)


def in_hbm(array):
    return pltpu.with_memory_space_constraint(array, pltpu.HBM)


def project_kernel(count, n_w, first, last, ids, core, *refs):
    xs, refs = refs[:count], refs[count:]
    ws, refs = refs[: n_w * count], refs[n_w * count :]
    if not first:
        acc, refs = refs[0], refs[1:]
    if last:
        sel_ref, ours, theirs = refs
    else:
        (out,) = refs
    parts = []
    for j in range(n_w):
        total = None if first else acc[:, j * WIDTH : (j + 1) * WIDTH]
        for i in range(count):
            term = jnp.dot(xs[i][...], ws[n_w * i + j][...], preferred_element_type=F32)
            total = term if total is None else total + term
        if last:
            parts.append(total.astype(BF16))
        else:
            out[:, j * WIDTH : (j + 1) * WIDTH] = total
    if last:
        columns = lax.broadcasted_iota(jnp.int32, (GMAX, ROWS), 1)
        pick = jnp.where(columns == sel_ref[...], 1.0, 0.0).astype(BF16)
        second = core[0] > 0
        for j, part in enumerate(parts):
            chosen = jnp.dot(pick, part, preferred_element_type=F32).astype(BF16)
            span = slice(j * HD, (j + 1) * HD)
            for rows, have in ((slice(0, ROWS), part), (slice(ROWS, UNIT), chosen)):
                left, right = have[:, :HD], have[:, HD:]
                ours[rows, span] = jnp.where(second, right, left)
                theirs[rows, span] = jnp.where(second, left, right)


def project(ids, core, offset, xs, weights, acc, selected=None):
    count, n_w = len(xs), len(weights)
    first, last = acc is None, selected is not None
    full = lambda shape: pl.BlockSpec(shape, lambda g, ids, core: (0, 0))
    in_specs = [full((ROWS, WIDTH)) for _ in xs]
    operands = list(xs)
    for i in range(count):
        for w in weights:
            in_specs.append(
                pl.BlockSpec(
                    (WIDTH, WIDTH), lambda g, ids, core, i=i: (ids[offset + i], 0)
                )
            )
            operands.append(in_hbm(w))
    aliases = {}
    if not first:
        in_specs.append(full((ROWS, n_w * WIDTH)))
        operands.append(acc)
        if not last:
            aliases = {len(operands) + 1: 0}
    if last:
        in_specs.append(full((GMAX, 1)))
        operands.append(selected)
        out_shape = (jax.ShapeDtypeStruct((UNIT, n_w * HD), BF16),) * 2
        out_specs = (full((UNIT, n_w * HD)),) * 2
    else:
        out_shape = jax.ShapeDtypeStruct((ROWS, n_w * WIDTH), F32)
        out_specs = full((ROWS, n_w * WIDTH))

    def body(*refs):
        project_kernel(count, n_w, first, last, *refs)

    return pl.pallas_call(
        body,
        out_shape=out_shape,
        grid_spec=pltpu.PrefetchScalarGridSpec(
            num_scalar_prefetch=2, grid=(1,), in_specs=in_specs, out_specs=out_specs
        ),
        input_output_aliases=aliases,
        compiler_params=pltpu.CompilerParams(vmem_limit_bytes=40 << 20),
        cost_estimate=pl.CostEstimate(
            flops=2 * count * ROWS * WIDTH * n_w * WIDTH,
            transcendentals=0,
            bytes_accessed=6 << 20,
        ),
        name="project",
    )(ids, core, *operands)


def combine_kernel(count, first, last, ids, odd, *refs):
    cs, refs = refs[:count], refs[count:]
    ws, refs = refs[: 4 * count], refs[4 * count :]
    flip = odd[0] > 0
    total = None
    if not first:
        acc, refs = refs[0], refs[1:]
        total = acc[...]
    (out,) = refs
    for i in range(count):
        quarters = [w[0] for w in ws[4 * i : 4 * i + 4]]
        w = jnp.concatenate(
            [
                jnp.where(flip, quarters[n ^ 1], quarters[n])
                for n in range(4)
            ],
            axis=0,
        )
        part = jnp.dot(cs[i][...], w, preferred_element_type=F32)
        part = part.astype(BF16).astype(F32)
        total = part if total is None else total + part
    out[...] = total.astype(out.dtype)


def combine(ids, odd, offset, cs, w_parts, acc, last=False):
    count = len(cs)
    first = acc is None
    full = lambda shape: pl.BlockSpec(shape, lambda g, ids, odd: (0, 0))
    in_specs = [full((ROWS, WIDTH)) for _ in cs]
    operands = list(cs)
    for i in range(count):
        for w in w_parts:
            in_specs.append(
                pl.BlockSpec(
                    (1, WIDTH // 4, WIDTH),
                    lambda g, ids, odd, i=i: (ids[offset + i], 0, 0),
                )
            )
            operands.append(in_hbm(w))
    aliases = {}
    if not first:
        in_specs.append(full((ROWS, WIDTH)))
        operands.append(acc)
        if not last:
            aliases = {len(operands) + 1: 0}

    def body(*refs):
        combine_kernel(count, first, last, *refs)

    return pl.pallas_call(
        body,
        out_shape=jax.ShapeDtypeStruct((ROWS, WIDTH), BF16 if last else F32),
        grid_spec=pltpu.PrefetchScalarGridSpec(
            num_scalar_prefetch=2,
            grid=(1,),
            in_specs=in_specs,
            out_specs=full((ROWS, WIDTH)),
        ),
        input_output_aliases=aliases,
        compiler_params=pltpu.CompilerParams(vmem_limit_bytes=40 << 20),
        cost_estimate=pl.CostEstimate(
            flops=2 * count * ROWS * WIDTH * WIDTH,
            transcendentals=0,
            bytes_accessed=3 << 20,
        ),
        name="combine",
    )(ids, odd, *operands)


def split_kernel(quarter, w_ref, out_ref):
    for j in range(N_HEADS):
        out_ref[j] = w_ref[:, j * WIDTH : (j + 1) * WIDTH]


def split_columns(quarter, w_out):
    rows = WIDTH // 4
    return pl.pallas_call(
        split_kernel,
        out_shape=jax.ShapeDtypeStruct((N_HEADS, rows, WIDTH), BF16),
        grid_spec=pltpu.PrefetchScalarGridSpec(
            num_scalar_prefetch=1,
            grid=(1,),
            in_specs=[
                pl.BlockSpec(
                    (rows, N_HEADS * WIDTH), lambda g, quarter: (quarter[0], 0)
                )
            ],
            out_specs=pl.BlockSpec(
                (N_HEADS, rows, WIDTH), lambda g, quarter: (0, 0, 0)
            ),
        ),
        cost_estimate=pl.CostEstimate(
            flops=0, transcendentals=0, bytes_accessed=1 << 20
        ),
        name="split_columns",
    )(quarter, in_hbm(w_out))


def gather_heads(own, work):
    have = {(0, 0): own}
    before = [own]
    state = None
    for t, (up, down, across) in enumerate(HEAD_SLOTS):
        ready = [have[up], have[down], have[across]]
        if state is not None:
            ready = [lax.optimization_barrier((item, state))[0] for item in ready]
        got = [
            lax.ppermute(ready[0], "heads", Z_UP),
            lax.ppermute(ready[1], "heads", Z_DOWN),
            lax.ppermute(ready[2], "heads", PAIR),
        ]
        state = work.state = work(t, before)
        have[(up[0] - 1, up[1])] = got[0]
        have[(down[0] + 1, down[1])] = got[1]
        have[(across[0], across[1] ^ 1)] = got[2]
        before = got
    return before


def gather_seq(mine, theirs):
    up = lambda a: lax.ppermute(a, "seq", Y_UP)
    down = lambda a: lax.ppermute(a, "seq", Y_DOWN)
    half = lambda a: lax.ppermute(a, "seq", HALF)
    near = ({(0, 0): mine}, {(0, 0): theirs})
    for n in near:
        n[0, 3] = up(n[0, 0])
        n[0, 1] = down(n[0, 0])
    a, b = near
    a[1, 0] = half(mine)
    b[1, 0] = half(theirs)
    for n in near:
        n[1, 3] = half(n[0, 3])
        n[0, 2] = up(n[0, 3])
        n[1, 1] = down(n[1, 0])
    near[0][1, 2] = up(near[0][1, 3])
    near[1][1, 2] = down(near[1][1, 1])
    return [near[slot % 2][slot // 8, slot // 2 % 4] for slot in range(N_SEQ)]


def attention_kernel(slots, rows, reach, *refs):
    queries, (gslot_ref, *sels), refs = refs[:2], refs[2:5], refs[5:]
    pieces, (*outs, buf, sems) = refs[:N_SEQ], refs[N_SEQ:]
    copies = [
        pltpu.make_async_copy(pieces[i], buf.at[i], sems.at[i]) for i in range(N_SEQ)
    ]
    for copy in copies:
        copy.start()
    for copy in copies:
        copy.wait()

    dims = (((1,), (1,)), ((), ()))

    def scored(q, k):
        return lax.dot_general(q, k, dims, preferred_element_type=F32) * SCALE

    found = jnp.concatenate([buf[i, ROWS:UNIT, :] for i in range(N_SEQ)], axis=0)
    where = lax.broadcasted_iota(jnp.int32, (G, N_SEQ * GMAX), 1)
    pick = jnp.where(where == gslot_ref[...], 1.0, 0.0).astype(BF16)
    g_kv = jnp.dot(pick, found, preferred_element_type=F32).astype(BF16)

    g_query = jnp.concatenate([q[ROWS:UNIT, :] for q in queries], axis=0)
    g_scores = [scored(g_query, buf[i, :ROWS, :HD]) for i in range(N_SEQ)]
    top = g_scores[0]
    for s in g_scores[1:]:
        top = jnp.maximum(top, s)
    top = jnp.max(top, axis=1, keepdims=True)
    sums = jnp.zeros((2 * GMAX, ROWS), F32)
    acc = jnp.zeros((2 * GMAX, HD), F32)
    for i in range(N_SEQ):
        p = jnp.exp(g_scores[i] - top)
        sums = sums + p
        acc = acc + jnp.dot(
            p.astype(BF16), buf[i, :ROWS, HD:], preferred_element_type=F32
        )
    g_context = (acc / jnp.sum(sums, axis=1, keepdims=True)).astype(BF16)

    wide = reach[0] >= WMAX
    for side in range(2):
        steps = lax.broadcasted_iota(jnp.int32, (ROWS, GMAX), 0)
        place = jnp.where(steps == sels[side][...], 1.0, 0.0)
        is_global = jnp.sum(place, axis=1, keepdims=True) > 0.5
        placed = jnp.dot(
            place.astype(BF16),
            g_context[side * GMAX : (side + 1) * GMAX],
            preferred_element_type=F32,
        )
        for b in range(BLK_DEV):
            span = slice(b * BLK, (b + 1) * BLK)
            query = queries[side][span, :]
            first = (side * BLK_DEV + b) * PICKS
            keys_at = [
                (slots[first + j], pl.ds(pl.multiple_of(rows[first + j], BLK), BLK))
                for j in range(PICKS)
            ]
            keys = [buf[slot, at, :HD] for slot, at in keys_at] + [g_kv[:, :HD]]
            values = [buf[slot, at, HD:] for slot, at in keys_at] + [g_kv[:, HD:]]
            scores = scored(query, jnp.concatenate(keys, axis=0))
            scores = [
                jnp.where(wide, scores[:, :BLK], NEGATIVE),
                scores[:, BLK : (SPAN - 1) * BLK],
                jnp.where(wide, scores[:, (SPAN - 1) * BLK : SPAN * BLK], NEGATIVE),
                scores[:, SPAN * BLK :],
            ]
            scores = jnp.concatenate(scores, axis=1)
            top = jnp.max(scores, axis=1, keepdims=True)
            p = jnp.exp(scores - top)
            acc = jnp.dot(
                p.astype(BF16),
                jnp.concatenate(values, axis=0),
                preferred_element_type=F32,
            )
            context = acc / jnp.sum(p, axis=1, keepdims=True)
            outs[side][span, :] = jnp.where(
                is_global[span], placed[span], context
            ).astype(BF16)


def attention(slots, rows, reach, queries, gslot, selected, pieces):
    return pl.pallas_call(
        attention_kernel,
        out_shape=(jax.ShapeDtypeStruct((ROWS, HD), BF16),) * 2,
        grid_spec=pltpu.PrefetchScalarGridSpec(
            num_scalar_prefetch=3,
            grid=(),
            in_specs=[vmem()] * 5
            + [pl.BlockSpec(memory_space=pl.ANY)] * len(pieces),
            out_specs=(vmem(),) * 2,
            scratch_shapes=[
                pltpu.VMEM((N_SEQ, UNIT, 2 * HD), BF16),
                pltpu.SemaphoreType.DMA((len(pieces),)),
            ],
        ),
        compiler_params=pltpu.CompilerParams(vmem_limit_bytes=48 << 20),
        cost_estimate=pl.CostEstimate(
            flops=2 << 30, transcendentals=3 << 20, bytes_accessed=8 << 20
        ),
        name="attention",
    )(slots, rows, reach, *queries, gslot, *selected, *[in_hbm(p) for p in pieces])


def on_device(
    activations, w_query, w_key, w_value, w_out, windows, rand_blocks, global_pos
):
    me = lax.axis_index("heads")
    here = lax.axis_index("seq")
    items = head_order()
    shifts = jnp.array([d for d, _ in items], jnp.int32)
    flips = jnp.array([e for _, e in items], jnp.int32)
    ids = (me // 2 + shifts + 8) % 8 * 2 + (me % 2 + flips) % 2

    def slot_of(seq):
        dx = (seq // 8 + here // 8) % 2
        dy = (seq // 2 % 4 - here // 2 % 4 + 4) % 4
        return dx * 8 + dy * 2 + (seq + here) % 2

    swap = lambda a: lax.ppermute(a, "seq", CORE)
    other = here + 1 - 2 * (here % 2)
    sides = jnp.stack([here, other])
    blocks = (
        sides[:, None] * BLK_DEV + jnp.arange(BLK_DEV, dtype=jnp.int32)[None, :]
    ).reshape(-1, 1)
    offsets = jnp.arange(SPAN, dtype=jnp.int32)[None, :] - WMAX
    near = (blocks + offsets + NBLK) % NBLK
    rand_there = swap(rand_blocks)

    owners = global_pos // ROWS
    order = jnp.arange(G, dtype=jnp.int32)
    earlier = (owners[:, None] == owners[None, :]) & (order[None, :] < order[:, None])
    ranks = jnp.sum(earlier.astype(jnp.int32), axis=1)
    gslot = (slot_of(owners) * GMAX + ranks)[:, None]
    local = owners[None, None, :] == sides[:, None, None]
    mine = local & (
        ranks[None, :] == jnp.arange(GMAX, dtype=jnp.int32)[:, None]
    )
    selected = jnp.max(jnp.where(mine, global_pos % ROWS, -1), axis=2)

    weights = (w_key, w_value)
    core = (here % 2)[None]
    odd = (here // 2 % 2)[None]

    shards = []

    class Projection:
        state = None

        def __call__(self, t, arrivals):
            shards.extend(arrivals)
            acc = self.state and self.state[0]
            acc = project(ids, core, max(3 * t - 2, 0), arrivals, weights, acc)
            if t == 1:
                return acc, split_columns(core * 2 + odd, w_out), rand_there
            return (acc, *self.state[1:]) if self.state else (acc,)

    projection = Projection()
    last = gather_heads(activations, projection)
    acc, w_blocks, rand_there = projection.state
    rand_there, acc = lax.optimization_barrier((rand_there, acc))
    picks = jnp.concatenate([rand_blocks, rand_there], axis=0)
    named = jnp.concatenate([near, picks], axis=1).reshape(-1)
    key_slots = slot_of(named // BLK_DEV)
    key_rows = named % BLK_DEV * BLK
    kv, kv_away = project(
        ids, core, 13, last, weights, acc, selected=selected[0][:, None]
    )
    query, query_away = project(
        ids,
        core,
        0,
        [in_hbm(x) for x in (*shards, *last)],
        (w_query,),
        None,
        selected=selected[0][:, None],
    )
    pieces = gather_seq(kv, swap(kv_away))
    query_here = swap(query_away)
    pieces, query_here, w_blocks = lax.optimization_barrier(
        (pieces, query_here, w_blocks)
    )
    w_quarter = lax.all_to_all(w_blocks, "heads", 0, 0)
    context, context_away = attention(
        key_slots,
        key_rows,
        jnp.where(core > 0, windows[1:], windows[:1]),
        (query, query_here),
        gslot,
        (selected[:1], selected[1:]),
        pieces,
    )
    context = jnp.concatenate([context, swap(context_away)], axis=1)
    context, w_quarter = lax.optimization_barrier((context, w_quarter))
    w_half = (w_quarter, lax.ppermute(w_quarter, "seq", Y_PAIR))
    w_parts = (*w_half, *(swap(w) for w in w_half))

    class Combination:
        state = None
        waiting = ()

        def __call__(self, t, arrivals):
            self.waiting = (*self.waiting, *arrivals)
            if t < 3:
                return self.state
            start = 3 * t + 1 - len(self.waiting)
            out = combine(
                ids, odd, start, self.waiting, w_parts, self.state, last=t == 5
            )
            self.waiting = ()
            return out

    combination = Combination()
    return combination(5, gather_heads(context, combination))


def solution(mesh):
    in_specs = (
        P("seq", "heads"),
        P(None, "heads"),
        P(None, "heads"),
        P(None, "heads"),
        P("heads", None),
        P("heads"),
        P("seq", None),
        P(),
    )
    out_specs = P("seq", "heads")
    return jax.shard_map(
        on_device, mesh=mesh, in_specs=in_specs, out_specs=out_specs, check_vma=False
    )
```

```python
import math

import jax
import jax.numpy as jnp
from jax import lax
from jax.experimental import pallas as pl
from jax.experimental.pallas import tpu as pltpu
from jax.sharding import PartitionSpec as P

WMAX = 2
SPAN = 2 * WMAX + 1
R = 3
PICKS = SPAN + R
BLK = 128
BLK_DEV = 6
ROWS = BLK * BLK_DEV
GMAX = 32
G = 128
HD = 128
HEADS_DEV = 2
WIDTH = HD * HEADS_DEV
N_SEQ = 16
N_HEADS = 16
NBLK = N_SEQ * BLK_DEV
UNIT = ROWS + GMAX
NEGATIVE = -1e30
SCALE = 1.0 / math.sqrt(HD)
F32 = jnp.float32
BF16 = jnp.bfloat16

HEAD_SLOTS = (
    ((0, 0), (0, 0), (0, 0)),
    ((-1, 0), (1, 0), (-1, 0)),
    ((-2, 0), (2, 0), (1, 0)),
    ((-3, 0), (1, 1), (-2, 0)),
    ((-2, 1), (2, 1), (-4, 0)),
)
Z_UP = [(h, (h + 2) % 16) for h in range(16)]
Z_DOWN = [(h, (h - 2) % 16) for h in range(16)]
PAIR = [(h, h ^ 1) for h in range(16)]


def head_order():
    items = [(0, 0)]
    for up, down, across in HEAD_SLOTS:
        items += [
            (up[0] - 1, up[1]),
            (down[0] + 1, down[1]),
            (across[0], across[1] ^ 1),
        ]
    return items


Y_UP = [(s, (s // 8) * 8 + (s % 8 + 2) % 8) for s in range(16)]
Y_DOWN = [(s, (s // 8) * 8 + (s % 8 - 2) % 8) for s in range(16)]
HALF = [(s, s ^ 8) for s in range(16)]
CORE = [(s, s ^ 1) for s in range(16)]
Y_PAIR = [(s, s ^ 2) for s in range(16)]


def vmem():
    return pl.BlockSpec(memory_space=pltpu.VMEM)


def in_hbm(array):
    return pltpu.with_memory_space_constraint(array, pltpu.HBM)


def project_kernel(count, n_w, first, last, ids, core, *refs):
    xs, refs = refs[:count], refs[count:]
    ws, refs = refs[: n_w * count], refs[n_w * count :]
    if not first:
        acc, refs = refs[0], refs[1:]
    if last:
        sel_ref, ours, theirs = refs
    else:
        (out,) = refs
    parts = []
    for j in range(n_w):
        total = None if first else acc[:, j * WIDTH : (j + 1) * WIDTH]
        for i in range(count):
            term = jnp.dot(xs[i][...], ws[n_w * i + j][...], preferred_element_type=F32)
            total = term if total is None else total + term
        if last:
            parts.append(total.astype(BF16))
        else:
            out[:, j * WIDTH : (j + 1) * WIDTH] = total
    if last:
        columns = lax.broadcasted_iota(jnp.int32, (GMAX, ROWS), 1)
        pick = jnp.where(columns == sel_ref[...], 1.0, 0.0).astype(BF16)
        second = core[0] > 0
        for j, part in enumerate(parts):
            chosen = jnp.dot(pick, part, preferred_element_type=F32).astype(BF16)
            span = slice(j * HD, (j + 1) * HD)
            for rows, have in ((slice(0, ROWS), part), (slice(ROWS, UNIT), chosen)):
                left, right = have[:, :HD], have[:, HD:]
                ours[rows, span] = jnp.where(second, right, left)
                theirs[rows, span] = jnp.where(second, left, right)


def project(ids, core, offset, xs, weights, acc, selected=None):
    count, n_w = len(xs), len(weights)
    first, last = acc is None, selected is not None
    full = lambda shape: pl.BlockSpec(shape, lambda g, ids, core: (0, 0))
    in_specs = [full((ROWS, WIDTH)) for _ in xs]
    operands = list(xs)
    for i in range(count):
        for w in weights:
            in_specs.append(
                pl.BlockSpec(
                    (WIDTH, WIDTH), lambda g, ids, core, i=i: (ids[offset + i], 0)
                )
            )
            operands.append(in_hbm(w))
    aliases = {}
    if not first:
        in_specs.append(full((ROWS, n_w * WIDTH)))
        operands.append(acc)
        if not last:
            aliases = {len(operands) + 1: 0}
    if last:
        in_specs.append(full((GMAX, 1)))
        operands.append(selected)
        out_shape = (jax.ShapeDtypeStruct((UNIT, n_w * HD), BF16),) * 2
        out_specs = (full((UNIT, n_w * HD)),) * 2
    else:
        out_shape = jax.ShapeDtypeStruct((ROWS, n_w * WIDTH), F32)
        out_specs = full((ROWS, n_w * WIDTH))

    def body(*refs):
        project_kernel(count, n_w, first, last, *refs)

    return pl.pallas_call(
        body,
        out_shape=out_shape,
        grid_spec=pltpu.PrefetchScalarGridSpec(
            num_scalar_prefetch=2, grid=(1,), in_specs=in_specs, out_specs=out_specs
        ),
        input_output_aliases=aliases,
        compiler_params=pltpu.CompilerParams(vmem_limit_bytes=40 << 20),
        cost_estimate=pl.CostEstimate(
            flops=2 * count * ROWS * WIDTH * n_w * WIDTH,
            transcendentals=0,
            bytes_accessed=6 << 20,
        ),
        name="project",
    )(ids, core, *operands)


def combine_kernel(count, first, last, ids, odd, *refs):
    cs, refs = refs[:count], refs[count:]
    ws, refs = refs[: 4 * count], refs[4 * count :]
    flip = odd[0] > 0
    total = None
    if not first:
        acc, refs = refs[0], refs[1:]
        total = acc[...]
    (out,) = refs
    for i in range(count):
        quarters = [w[0] for w in ws[4 * i : 4 * i + 4]]
        w = jnp.concatenate(
            [
                jnp.where(flip, quarters[n ^ 1], quarters[n])
                for n in range(4)
            ],
            axis=0,
        )
        part = jnp.dot(cs[i][...], w, preferred_element_type=F32)
        part = part.astype(BF16).astype(F32)
        total = part if total is None else total + part
    out[...] = total.astype(out.dtype)


def combine(ids, odd, offset, cs, w_parts, acc, last=False):
    count = len(cs)
    first = acc is None
    full = lambda shape: pl.BlockSpec(shape, lambda g, ids, odd: (0, 0))
    in_specs = [full((ROWS, WIDTH)) for _ in cs]
    operands = list(cs)
    for i in range(count):
        for w in w_parts:
            in_specs.append(
                pl.BlockSpec(
                    (1, WIDTH // 4, WIDTH),
                    lambda g, ids, odd, i=i: (ids[offset + i], 0, 0),
                )
            )
            operands.append(in_hbm(w))
    aliases = {}
    if not first:
        in_specs.append(full((ROWS, WIDTH)))
        operands.append(acc)
        if not last:
            aliases = {len(operands) + 1: 0}

    def body(*refs):
        combine_kernel(count, first, last, *refs)

    return pl.pallas_call(
        body,
        out_shape=jax.ShapeDtypeStruct((ROWS, WIDTH), BF16 if last else F32),
        grid_spec=pltpu.PrefetchScalarGridSpec(
            num_scalar_prefetch=2,
            grid=(1,),
            in_specs=in_specs,
            out_specs=full((ROWS, WIDTH)),
        ),
        input_output_aliases=aliases,
        compiler_params=pltpu.CompilerParams(vmem_limit_bytes=40 << 20),
        cost_estimate=pl.CostEstimate(
            flops=2 * count * ROWS * WIDTH * WIDTH,
            transcendentals=0,
            bytes_accessed=3 << 20,
        ),
        name="combine",
    )(ids, odd, *operands)


def split_kernel(quarter, w_ref, out_ref):
    for j in range(N_HEADS):
        out_ref[j] = w_ref[:, j * WIDTH : (j + 1) * WIDTH]


def split_columns(quarter, w_out):
    rows = WIDTH // 4
    return pl.pallas_call(
        split_kernel,
        out_shape=jax.ShapeDtypeStruct((N_HEADS, rows, WIDTH), BF16),
        grid_spec=pltpu.PrefetchScalarGridSpec(
            num_scalar_prefetch=1,
            grid=(1,),
            in_specs=[
                pl.BlockSpec(
                    (rows, N_HEADS * WIDTH), lambda g, quarter: (quarter[0], 0)
                )
            ],
            out_specs=pl.BlockSpec(
                (N_HEADS, rows, WIDTH), lambda g, quarter: (0, 0, 0)
            ),
        ),
        cost_estimate=pl.CostEstimate(
            flops=0, transcendentals=0, bytes_accessed=1 << 20
        ),
        name="split_columns",
    )(quarter, in_hbm(w_out))


def gather_heads(own, work):
    have = {(0, 0): own}
    before = [own]
    state = None
    for t, (up, down, across) in enumerate(HEAD_SLOTS):
        ready = [have[up], have[down], have[across]]
        if state is not None:
            ready = [lax.optimization_barrier((item, state))[0] for item in ready]
        got = [
            lax.ppermute(ready[0], "heads", Z_UP),
            lax.ppermute(ready[1], "heads", Z_DOWN),
            lax.ppermute(ready[2], "heads", PAIR),
        ]
        state = work.state = work(t, before)
        have[(up[0] - 1, up[1])] = got[0]
        have[(down[0] + 1, down[1])] = got[1]
        have[(across[0], across[1] ^ 1)] = got[2]
        before = got
    return before


def gather_seq(mine, theirs):
    up = lambda a: lax.ppermute(a, "seq", Y_UP)
    down = lambda a: lax.ppermute(a, "seq", Y_DOWN)
    half = lambda a: lax.ppermute(a, "seq", HALF)
    near = ({(0, 0): mine}, {(0, 0): theirs})
    for n in near:
        n[0, 3] = up(n[0, 0])
        n[0, 1] = down(n[0, 0])
    a, b = near
    a[1, 0] = half(mine)
    b[1, 0] = half(theirs)
    for n in near:
        n[1, 3] = half(n[0, 3])
        n[0, 2] = up(n[0, 3])
        n[1, 1] = down(n[1, 0])
    near[0][1, 2] = up(near[0][1, 3])
    near[1][1, 2] = down(near[1][1, 1])
    return [near[slot % 2][slot // 8, slot // 2 % 4] for slot in range(N_SEQ)]


def attention_kernel(slots, rows, reach, *refs):
    queries, (gslot_ref, *sels), refs = refs[:2], refs[2:5], refs[5:]
    pieces, (*outs, buf, sems) = refs[:N_SEQ], refs[N_SEQ:]
    copies = [
        pltpu.make_async_copy(pieces[i], buf.at[i], sems.at[i]) for i in range(N_SEQ)
    ]
    for copy in copies:
        copy.start()
    for copy in copies:
        copy.wait()

    dims = (((1,), (1,)), ((), ()))

    def scored(q, k):
        return lax.dot_general(q, k, dims, preferred_element_type=F32) * SCALE

    found = jnp.concatenate([buf[i, ROWS:UNIT, :] for i in range(N_SEQ)], axis=0)
    where = lax.broadcasted_iota(jnp.int32, (G, N_SEQ * GMAX), 1)
    pick = jnp.where(where == gslot_ref[...], 1.0, 0.0).astype(BF16)
    g_kv = jnp.dot(pick, found, preferred_element_type=F32).astype(BF16)

    g_query = jnp.concatenate([q[ROWS:UNIT, :] for q in queries], axis=0)
    g_scores = [scored(g_query, buf[i, :ROWS, :HD]) for i in range(N_SEQ)]
    top = g_scores[0]
    for s in g_scores[1:]:
        top = jnp.maximum(top, s)
    top = jnp.max(top, axis=1, keepdims=True)
    sums = jnp.zeros((2 * GMAX, ROWS), F32)
    acc = jnp.zeros((2 * GMAX, HD), F32)
    for i in range(N_SEQ):
        p = jnp.exp(g_scores[i] - top)
        sums = sums + p
        acc = acc + jnp.dot(
            p.astype(BF16), buf[i, :ROWS, HD:], preferred_element_type=F32
        )
    g_context = (acc / jnp.sum(sums, axis=1, keepdims=True)).astype(BF16)

    wide = reach[0] >= WMAX
    for side in range(2):
        steps = lax.broadcasted_iota(jnp.int32, (ROWS, GMAX), 0)
        place = jnp.where(steps == sels[side][...], 1.0, 0.0)
        is_global = jnp.sum(place, axis=1, keepdims=True) > 0.5
        placed = jnp.dot(
            place.astype(BF16),
            g_context[side * GMAX : (side + 1) * GMAX],
            preferred_element_type=F32,
        )
        for b in range(BLK_DEV):
            span = slice(b * BLK, (b + 1) * BLK)
            query = queries[side][span, :]
            first = (side * BLK_DEV + b) * PICKS
            keys_at = [
                (slots[first + j], pl.ds(pl.multiple_of(rows[first + j], BLK), BLK))
                for j in range(PICKS)
            ]
            keys = [buf[slot, at, :HD] for slot, at in keys_at] + [g_kv[:, :HD]]
            values = [buf[slot, at, HD:] for slot, at in keys_at] + [g_kv[:, HD:]]
            scores = scored(query, jnp.concatenate(keys, axis=0))
            scores = [
                jnp.where(wide, scores[:, :BLK], NEGATIVE),
                scores[:, BLK : (SPAN - 1) * BLK],
                jnp.where(wide, scores[:, (SPAN - 1) * BLK : SPAN * BLK], NEGATIVE),
                scores[:, SPAN * BLK :],
            ]
            scores = jnp.concatenate(scores, axis=1)
            top = jnp.max(scores, axis=1, keepdims=True)
            p = jnp.exp(scores - top)
            acc = jnp.dot(
                p.astype(BF16),
                jnp.concatenate(values, axis=0),
                preferred_element_type=F32,
            )
            context = acc / jnp.sum(p, axis=1, keepdims=True)
            outs[side][span, :] = jnp.where(
                is_global[span], placed[span], context
            ).astype(BF16)


def attention(slots, rows, reach, queries, gslot, selected, pieces):
    return pl.pallas_call(
        attention_kernel,
        out_shape=(jax.ShapeDtypeStruct((ROWS, HD), BF16),) * 2,
        grid_spec=pltpu.PrefetchScalarGridSpec(
            num_scalar_prefetch=3,
            grid=(),
            in_specs=[vmem()] * 5
            + [pl.BlockSpec(memory_space=pl.ANY)] * len(pieces),
            out_specs=(vmem(),) * 2,
            scratch_shapes=[
                pltpu.VMEM((N_SEQ, UNIT, 2 * HD), BF16),
                pltpu.SemaphoreType.DMA((len(pieces),)),
            ],
        ),
        compiler_params=pltpu.CompilerParams(vmem_limit_bytes=48 << 20),
        cost_estimate=pl.CostEstimate(
            flops=2 << 30, transcendentals=3 << 20, bytes_accessed=8 << 20
        ),
        name="attention",
    )(slots, rows, reach, *queries, gslot, *selected, *[in_hbm(p) for p in pieces])


def on_device(
    activations, w_query, w_key, w_value, w_out, windows, rand_blocks, global_pos
):
    me = lax.axis_index("heads")
    here = lax.axis_index("seq")
    items = head_order()
    shifts = jnp.array([d for d, _ in items], jnp.int32)
    flips = jnp.array([e for _, e in items], jnp.int32)
    ids = (me // 2 + shifts + 8) % 8 * 2 + (me % 2 + flips) % 2

    def slot_of(seq):
        dx = (seq // 8 + here // 8) % 2
        dy = (seq // 2 % 4 - here // 2 % 4 + 4) % 4
        return dx * 8 + dy * 2 + (seq + here) % 2

    swap = lambda a: lax.ppermute(a, "seq", CORE)
    other = here + 1 - 2 * (here % 2)
    sides = jnp.stack([here, other])
    blocks = (
        sides[:, None] * BLK_DEV + jnp.arange(BLK_DEV, dtype=jnp.int32)[None, :]
    ).reshape(-1, 1)
    offsets = jnp.arange(SPAN, dtype=jnp.int32)[None, :] - WMAX
    near = (blocks + offsets + NBLK) % NBLK
    rand_there = swap(rand_blocks)

    owners = global_pos // ROWS
    order = jnp.arange(G, dtype=jnp.int32)
    earlier = (owners[:, None] == owners[None, :]) & (order[None, :] < order[:, None])
    ranks = jnp.sum(earlier.astype(jnp.int32), axis=1)
    gslot = (slot_of(owners) * GMAX + ranks)[:, None]
    local = owners[None, None, :] == sides[:, None, None]
    mine = local & (
        ranks[None, :] == jnp.arange(GMAX, dtype=jnp.int32)[:, None]
    )
    selected = jnp.max(jnp.where(mine, global_pos % ROWS, -1), axis=2)

    weights = (w_key, w_value)
    core = (here % 2)[None]
    odd = (here // 2 % 2)[None]

    shards = []

    class Projection:
        state = None

        def __call__(self, t, arrivals):
            shards.extend(arrivals)
            acc = self.state and self.state[0]
            acc = project(ids, core, max(3 * t - 2, 0), arrivals, weights, acc)
            if t == 0:
                w_blocks = split_columns(core * 2 + odd, w_out)
                acc, w_blocks = lax.optimization_barrier((acc, w_blocks))
                self.moved = lax.all_to_all(w_blocks, "heads", 0, 0)
            if t == 3:
                return acc, self.moved
            return (acc, *self.state[1:]) if self.state else (acc,)

    projection = Projection()
    last = gather_heads(activations, projection)
    acc, w_quarter = projection.state
    rand_there, acc = lax.optimization_barrier((rand_there, acc))
    picks = jnp.concatenate([rand_blocks, rand_there], axis=0)
    named = jnp.concatenate([near, picks], axis=1).reshape(-1)
    key_slots = slot_of(named // BLK_DEV)
    key_rows = named % BLK_DEV * BLK
    kv, kv_away = project(
        ids, core, 13, last, weights, acc, selected=selected[0][:, None]
    )
    query, query_away = project(
        ids,
        core,
        0,
        [in_hbm(x) for x in (*shards, *last)],
        (w_query,),
        None,
        selected=selected[0][:, None],
    )
    pieces = gather_seq(kv, swap(kv_away))
    query_here = swap(query_away)
    query_here, pieces[2] = lax.optimization_barrier((query_here, pieces[2]))
    pieces, w_quarter = lax.optimization_barrier((pieces, w_quarter))
    w_half = (w_quarter, lax.ppermute(w_quarter, "seq", Y_PAIR))
    context, context_away = attention(
        key_slots,
        key_rows,
        jnp.where(core > 0, windows[1:], windows[:1]),
        (query, query_here),
        gslot,
        (selected[:1], selected[1:]),
        pieces,
    )
    context = jnp.concatenate([context, swap(context_away)], axis=1)
    context, w_half = lax.optimization_barrier((context, w_half))
    w_parts = (*w_half, *(swap(w) for w in w_half))

    class Combination:
        state = None
        waiting = ()

        def __call__(self, t, arrivals):
            self.waiting = (*self.waiting, *arrivals)
            if t < 2:
                return self.state
            start = 3 * t + 1 - len(self.waiting)
            out = combine(
                ids, odd, start, self.waiting, w_parts, self.state, last=t == 5
            )
            self.waiting = ()
            return out

    combination = Combination()
    return combination(5, gather_heads(context, combination))


def solution(mesh):
    in_specs = (
        P("seq", "heads"),
        P(None, "heads"),
        P(None, "heads"),
        P(None, "heads"),
        P("heads", None),
        P("heads"),
        P("seq", None),
        P(),
    )
    out_specs = P("seq", "heads")
    return jax.shard_map(
        on_device, mesh=mesh, in_specs=in_specs, out_specs=out_specs, check_vma=False
    )
```

```python
import math

import jax
import jax.numpy as jnp
from jax import lax
from jax.experimental import pallas as pl
from jax.experimental.pallas import tpu as pltpu
from jax.sharding import PartitionSpec as P

WMAX = 2
SPAN = 2 * WMAX + 1
R = 3
PICKS = SPAN + R
BLK = 128
BLK_DEV = 6
ROWS = BLK * BLK_DEV
GMAX = 32
G = 128
HD = 128
HEADS_DEV = 2
WIDTH = HD * HEADS_DEV
N_SEQ = 16
N_HEADS = 16
NBLK = N_SEQ * BLK_DEV
UNIT = ROWS + GMAX
NEGATIVE = -1e30
SCALE = 1.0 / math.sqrt(HD)
F32 = jnp.float32
BF16 = jnp.bfloat16

HEAD_SLOTS = (
    ((0, 0), (0, 0), (0, 0)),
    ((-1, 0), (1, 0), (-1, 0)),
    ((-2, 0), (2, 0), (2, 0)),
    ((-3, 0), (2, 1), (-2, 0)),
    ((-2, 1), (3, 1), (1, 0)),
)
Z_UP = [(h, (h + 2) % 16) for h in range(16)]
Z_DOWN = [(h, (h - 2) % 16) for h in range(16)]
PAIR = [(h, h ^ 1) for h in range(16)]


def head_order():
    items = [(0, 0)]
    for up, down, across in HEAD_SLOTS:
        items += [
            (up[0] - 1, up[1]),
            (down[0] + 1, down[1]),
            (across[0], across[1] ^ 1),
        ]
    return items


Y_UP = [(s, (s // 8) * 8 + (s % 8 + 2) % 8) for s in range(16)]
Y_DOWN = [(s, (s // 8) * 8 + (s % 8 - 2) % 8) for s in range(16)]
HALF = [(s, s ^ 8) for s in range(16)]
CORE = [(s, s ^ 1) for s in range(16)]
Y_PAIR = [(s, s ^ 2) for s in range(16)]


def vmem():
    return pl.BlockSpec(memory_space=pltpu.VMEM)


def in_hbm(array):
    return pltpu.with_memory_space_constraint(array, pltpu.HBM)


def project_kernel(count, n_w, first, last, ids, core, *refs):
    xs, refs = refs[:count], refs[count:]
    ws, refs = refs[: n_w * count], refs[n_w * count :]
    if not first:
        acc, refs = refs[0], refs[1:]
    if last:
        sel_ref, ours, theirs = refs
    else:
        (out,) = refs
    parts = []
    for j in range(n_w):
        total = None if first else acc[:, j * WIDTH : (j + 1) * WIDTH]
        for i in range(count):
            term = jnp.dot(xs[i][...], ws[n_w * i + j][...], preferred_element_type=F32)
            total = term if total is None else total + term
        if last:
            parts.append(total.astype(BF16))
        else:
            out[:, j * WIDTH : (j + 1) * WIDTH] = total
    if last:
        columns = lax.broadcasted_iota(jnp.int32, (GMAX, ROWS), 1)
        pick = jnp.where(columns == sel_ref[...], 1.0, 0.0).astype(BF16)
        second = core[0] > 0
        for j, part in enumerate(parts):
            chosen = jnp.dot(pick, part, preferred_element_type=F32).astype(BF16)
            span = slice(j * HD, (j + 1) * HD)
            for rows, have in ((slice(0, ROWS), part), (slice(ROWS, UNIT), chosen)):
                left, right = have[:, :HD], have[:, HD:]
                ours[rows, span] = jnp.where(second, right, left)
                theirs[rows, span] = jnp.where(second, left, right)


def project(ids, core, offset, xs, weights, acc, selected=None):
    count, n_w = len(xs), len(weights)
    first, last = acc is None, selected is not None
    full = lambda shape: pl.BlockSpec(shape, lambda g, ids, core: (0, 0))
    in_specs = [full((ROWS, WIDTH)) for _ in xs]
    operands = list(xs)
    for i in range(count):
        for w in weights:
            in_specs.append(
                pl.BlockSpec(
                    (WIDTH, WIDTH), lambda g, ids, core, i=i: (ids[offset + i], 0)
                )
            )
            operands.append(in_hbm(w))
    aliases = {}
    if not first:
        in_specs.append(full((ROWS, n_w * WIDTH)))
        operands.append(acc)
        if not last:
            aliases = {len(operands) + 1: 0}
    if last:
        in_specs.append(full((GMAX, 1)))
        operands.append(selected)
        out_shape = (jax.ShapeDtypeStruct((UNIT, n_w * HD), BF16),) * 2
        out_specs = (full((UNIT, n_w * HD)),) * 2
    else:
        out_shape = jax.ShapeDtypeStruct((ROWS, n_w * WIDTH), F32)
        out_specs = full((ROWS, n_w * WIDTH))

    def body(*refs):
        project_kernel(count, n_w, first, last, *refs)

    return pl.pallas_call(
        body,
        out_shape=out_shape,
        grid_spec=pltpu.PrefetchScalarGridSpec(
            num_scalar_prefetch=2, grid=(1,), in_specs=in_specs, out_specs=out_specs
        ),
        input_output_aliases=aliases,
        compiler_params=pltpu.CompilerParams(vmem_limit_bytes=40 << 20),
        cost_estimate=pl.CostEstimate(
            flops=2 * count * ROWS * WIDTH * n_w * WIDTH,
            transcendentals=0,
            bytes_accessed=6 << 20,
        ),
        name="project",
    )(ids, core, *operands)


def combine_kernel(count, first, last, ids, odd, *refs):
    cs, refs = refs[:count], refs[count:]
    ws, refs = refs[: 4 * count], refs[4 * count :]
    flip = odd[0] > 0
    total = None
    if not first:
        acc, refs = refs[0], refs[1:]
        total = acc[...]
    (out,) = refs
    for i in range(count):
        quarters = [w[0] for w in ws[4 * i : 4 * i + 4]]
        w = jnp.concatenate(
            [
                jnp.where(flip, quarters[n ^ 1], quarters[n])
                for n in range(4)
            ],
            axis=0,
        )
        part = jnp.dot(cs[i][...], w, preferred_element_type=F32)
        part = part.astype(BF16).astype(F32)
        total = part if total is None else total + part
    out[...] = total.astype(out.dtype)


def combine(ids, odd, offset, cs, w_parts, acc, last=False):
    count = len(cs)
    first = acc is None
    full = lambda shape: pl.BlockSpec(shape, lambda g, ids, odd: (0, 0))
    in_specs = [full((ROWS, WIDTH)) for _ in cs]
    operands = list(cs)
    for i in range(count):
        for w in w_parts:
            in_specs.append(
                pl.BlockSpec(
                    (1, WIDTH // 4, WIDTH),
                    lambda g, ids, odd, i=i: (ids[offset + i], 0, 0),
                )
            )
            operands.append(in_hbm(w))
    aliases = {}
    if not first:
        in_specs.append(full((ROWS, WIDTH)))
        operands.append(acc)
        if not last:
            aliases = {len(operands) + 1: 0}

    def body(*refs):
        combine_kernel(count, first, last, *refs)

    return pl.pallas_call(
        body,
        out_shape=jax.ShapeDtypeStruct((ROWS, WIDTH), BF16 if last else F32),
        grid_spec=pltpu.PrefetchScalarGridSpec(
            num_scalar_prefetch=2,
            grid=(1,),
            in_specs=in_specs,
            out_specs=full((ROWS, WIDTH)),
        ),
        input_output_aliases=aliases,
        compiler_params=pltpu.CompilerParams(vmem_limit_bytes=40 << 20),
        cost_estimate=pl.CostEstimate(
            flops=2 * count * ROWS * WIDTH * WIDTH,
            transcendentals=0,
            bytes_accessed=3 << 20,
        ),
        name="combine",
    )(ids, odd, *operands)


def split_kernel(quarter, w_ref, out_ref):
    for j in range(N_HEADS):
        out_ref[j] = w_ref[:, j * WIDTH : (j + 1) * WIDTH]


def split_columns(quarter, w_out):
    rows = WIDTH // 4
    return pl.pallas_call(
        split_kernel,
        out_shape=jax.ShapeDtypeStruct((N_HEADS, rows, WIDTH), BF16),
        grid_spec=pltpu.PrefetchScalarGridSpec(
            num_scalar_prefetch=1,
            grid=(1,),
            in_specs=[
                pl.BlockSpec(
                    (rows, N_HEADS * WIDTH), lambda g, quarter: (quarter[0], 0)
                )
            ],
            out_specs=pl.BlockSpec(
                (N_HEADS, rows, WIDTH), lambda g, quarter: (0, 0, 0)
            ),
        ),
        cost_estimate=pl.CostEstimate(
            flops=0, transcendentals=0, bytes_accessed=1 << 20
        ),
        name="split_columns",
    )(quarter, in_hbm(w_out))


def gather_heads(own, work):
    have = {(0, 0): own}
    before = [own]
    state = None
    for t, (up, down, across) in enumerate(HEAD_SLOTS):
        ready = [have[up], have[down], have[across]]
        if state is not None:
            ready = [lax.optimization_barrier((item, state))[0] for item in ready]
        got = [
            lax.ppermute(ready[0], "heads", Z_UP),
            lax.ppermute(ready[1], "heads", Z_DOWN),
            lax.ppermute(ready[2], "heads", PAIR),
        ]
        state = work.state = work(t, before)
        have[(up[0] - 1, up[1])] = got[0]
        have[(down[0] + 1, down[1])] = got[1]
        have[(across[0], across[1] ^ 1)] = got[2]
        before = got
    return before


def gather_seq(mine, theirs):
    up = lambda a: lax.ppermute(a, "seq", Y_UP)
    down = lambda a: lax.ppermute(a, "seq", Y_DOWN)
    half = lambda a: lax.ppermute(a, "seq", HALF)
    near = ({(0, 0): mine}, {(0, 0): theirs})
    for n in near:
        n[1, 0] = half(n[0, 0])
        n[0, 3] = up(n[0, 0])
        n[0, 1] = down(n[0, 0])
    for n in near:
        n[1, 3] = half(n[0, 3])
        n[0, 2] = up(n[0, 3])
        n[1, 1] = down(n[1, 0])
    near[0][1, 2] = up(near[0][1, 3])
    near[1][1, 2] = down(near[1][1, 1])
    return [near[slot % 2][slot // 8, slot // 2 % 4] for slot in range(N_SEQ)]


def attention_kernel(slots, rows, reach, *refs):
    queries, (gslot_ref, *sels), refs = refs[:2], refs[2:5], refs[5:]
    pieces, (*outs, buf, sems) = refs[:N_SEQ], refs[N_SEQ:]
    copies = [
        pltpu.make_async_copy(pieces[i], buf.at[i], sems.at[i]) for i in range(N_SEQ)
    ]
    for copy in copies:
        copy.start()
    for copy in copies:
        copy.wait()

    dims = (((1,), (1,)), ((), ()))

    def scored(q, k):
        return lax.dot_general(q, k, dims, preferred_element_type=F32) * SCALE

    found = jnp.concatenate([buf[i, ROWS:UNIT, :] for i in range(N_SEQ)], axis=0)
    where = lax.broadcasted_iota(jnp.int32, (G, N_SEQ * GMAX), 1)
    pick = jnp.where(where == gslot_ref[...], 1.0, 0.0).astype(BF16)
    g_kv = jnp.dot(pick, found, preferred_element_type=F32).astype(BF16)

    g_query = jnp.concatenate([q[ROWS:UNIT, :] for q in queries], axis=0)
    g_scores = [scored(g_query, buf[i, :ROWS, :HD]) for i in range(N_SEQ)]
    top = g_scores[0]
    for s in g_scores[1:]:
        top = jnp.maximum(top, s)
    top = jnp.max(top, axis=1, keepdims=True)
    sums = jnp.zeros((2 * GMAX, ROWS), F32)
    acc = jnp.zeros((2 * GMAX, HD), F32)
    for i in range(N_SEQ):
        p = jnp.exp(g_scores[i] - top)
        sums = sums + p
        acc = acc + jnp.dot(
            p.astype(BF16), buf[i, :ROWS, HD:], preferred_element_type=F32
        )
    g_context = (acc / jnp.sum(sums, axis=1, keepdims=True)).astype(BF16)

    wide = reach[0] >= WMAX
    for side in range(2):
        steps = lax.broadcasted_iota(jnp.int32, (ROWS, GMAX), 0)
        place = jnp.where(steps == sels[side][...], 1.0, 0.0)
        is_global = jnp.sum(place, axis=1, keepdims=True) > 0.5
        placed = jnp.dot(
            place.astype(BF16),
            g_context[side * GMAX : (side + 1) * GMAX],
            preferred_element_type=F32,
        )
        for b in range(BLK_DEV):
            span = slice(b * BLK, (b + 1) * BLK)
            query = queries[side][span, :]
            first = (side * BLK_DEV + b) * PICKS
            keys_at = [
                (slots[first + j], pl.ds(pl.multiple_of(rows[first + j], BLK), BLK))
                for j in range(PICKS)
            ]
            keys = [buf[slot, at, :HD] for slot, at in keys_at] + [g_kv[:, :HD]]
            values = [buf[slot, at, HD:] for slot, at in keys_at] + [g_kv[:, HD:]]
            scores = scored(query, jnp.concatenate(keys, axis=0))
            scores = [
                jnp.where(wide, scores[:, :BLK], NEGATIVE),
                scores[:, BLK : (SPAN - 1) * BLK],
                jnp.where(wide, scores[:, (SPAN - 1) * BLK : SPAN * BLK], NEGATIVE),
                scores[:, SPAN * BLK :],
            ]
            scores = jnp.concatenate(scores, axis=1)
            top = jnp.max(scores, axis=1, keepdims=True)
            p = jnp.exp(scores - top)
            acc = jnp.dot(
                p.astype(BF16),
                jnp.concatenate(values, axis=0),
                preferred_element_type=F32,
            )
            context = acc / jnp.sum(p, axis=1, keepdims=True)
            outs[side][span, :] = jnp.where(
                is_global[span], placed[span], context
            ).astype(BF16)


def attention(slots, rows, reach, queries, gslot, selected, pieces):
    return pl.pallas_call(
        attention_kernel,
        out_shape=(jax.ShapeDtypeStruct((ROWS, HD), BF16),) * 2,
        grid_spec=pltpu.PrefetchScalarGridSpec(
            num_scalar_prefetch=3,
            grid=(),
            in_specs=[vmem()] * 5
            + [pl.BlockSpec(memory_space=pl.ANY)] * len(pieces),
            out_specs=(vmem(),) * 2,
            scratch_shapes=[
                pltpu.VMEM((N_SEQ, UNIT, 2 * HD), BF16),
                pltpu.SemaphoreType.DMA((len(pieces),)),
            ],
        ),
        compiler_params=pltpu.CompilerParams(vmem_limit_bytes=48 << 20),
        cost_estimate=pl.CostEstimate(
            flops=2 << 30, transcendentals=3 << 20, bytes_accessed=8 << 20
        ),
        name="attention",
    )(slots, rows, reach, *queries, gslot, *selected, *[in_hbm(p) for p in pieces])


def on_device(
    activations, w_query, w_key, w_value, w_out, windows, rand_blocks, global_pos
):
    me = lax.axis_index("heads")
    here = lax.axis_index("seq")
    items = head_order()
    shifts = jnp.array([d for d, _ in items], jnp.int32)
    flips = jnp.array([e for _, e in items], jnp.int32)
    ids = (me // 2 + shifts + 8) % 8 * 2 + (me % 2 + flips) % 2

    def slot_of(seq):
        dx = (seq // 8 + here // 8) % 2
        dy = (seq // 2 % 4 - here // 2 % 4 + 4) % 4
        return dx * 8 + dy * 2 + (seq + here) % 2

    swap = lambda a: lax.ppermute(a, "seq", CORE)
    other = here + 1 - 2 * (here % 2)
    sides = jnp.stack([here, other])
    blocks = (
        sides[:, None] * BLK_DEV + jnp.arange(BLK_DEV, dtype=jnp.int32)[None, :]
    ).reshape(-1, 1)
    offsets = jnp.arange(SPAN, dtype=jnp.int32)[None, :] - WMAX
    near = (blocks + offsets + NBLK) % NBLK
    picks = jnp.concatenate([rand_blocks, swap(rand_blocks)], axis=0)
    named = jnp.concatenate([near, picks], axis=1).reshape(-1)
    key_slots = slot_of(named // BLK_DEV)
    key_rows = named % BLK_DEV * BLK

    owners = global_pos // ROWS
    order = jnp.arange(G, dtype=jnp.int32)
    earlier = (owners[:, None] == owners[None, :]) & (order[None, :] < order[:, None])
    ranks = jnp.sum(earlier.astype(jnp.int32), axis=1)
    gslot = (slot_of(owners) * GMAX + ranks)[:, None]
    local = owners[None, None, :] == sides[:, None, None]
    mine = local & (
        ranks[None, :] == jnp.arange(GMAX, dtype=jnp.int32)[:, None]
    )
    selected = jnp.max(jnp.where(mine, global_pos % ROWS, -1), axis=2)

    weights = (w_key, w_value)
    core = (here % 2)[None]
    odd = (here // 2 % 2)[None]

    shards = []

    class Projection:
        state = None

        def __call__(self, t, arrivals):
            shards.extend(arrivals)
            acc = self.state and self.state[0]
            acc = project(ids, core, max(3 * t - 2, 0), arrivals, weights, acc)
            if t == 1:
                return acc, split_columns(core * 2 + odd, w_out)
            return (acc, *self.state[1:]) if self.state else (acc,)

    projection = Projection()
    last = gather_heads(activations, projection)
    acc, w_blocks = projection.state
    kv, kv_away = project(
        ids, core, 13, last, weights, acc, selected=selected[0][:, None]
    )
    query, query_away = project(
        ids,
        core,
        0,
        [*shards, *last],
        (w_query,),
        None,
        selected=selected[0][:, None],
    )
    pieces = gather_seq(kv, swap(kv_away))
    query_here = swap(query_away)
    pieces[6], w_blocks = lax.optimization_barrier((pieces[6], w_blocks))
    w_quarter = lax.all_to_all(w_blocks, "heads", 0, 0)
    pieces, w_quarter = lax.optimization_barrier((pieces, w_quarter))
    w_half = (w_quarter, lax.ppermute(w_quarter, "seq", Y_PAIR))
    context, context_away = attention(
        key_slots,
        key_rows,
        jnp.where(core > 0, windows[1:], windows[:1]),
        (query, query_here),
        gslot,
        (selected[:1], selected[1:]),
        pieces,
    )
    context = jnp.concatenate([context, swap(context_away)], axis=1)
    context, w_half = lax.optimization_barrier((context, w_half))
    w_parts = (*w_half, *(swap(w) for w in w_half))

    class Combination:
        state = None
        waiting = ()

        def __call__(self, t, arrivals):
            self.waiting = (*self.waiting, *arrivals)
            if t < 2:
                return self.state
            start = 3 * t + 1 - len(self.waiting)
            out = combine(
                ids, odd, start, self.waiting, w_parts, self.state, last=t == 5
            )
            self.waiting = ()
            return out

    combination = Combination()
    return combination(5, gather_heads(context, combination))


def solution(mesh):
    in_specs = (
        P("seq", "heads"),
        P(None, "heads"),
        P(None, "heads"),
        P(None, "heads"),
        P("heads", None),
        P("heads"),
        P("seq", None),
        P(),
    )
    out_specs = P("seq", "heads")
    return jax.shard_map(
        on_device, mesh=mesh, in_specs=in_specs, out_specs=out_specs, check_vma=False
    )
```

```python
import math

import jax
import jax.numpy as jnp
from jax import lax
from jax.experimental import pallas as pl
from jax.experimental.pallas import tpu as pltpu
from jax.sharding import PartitionSpec as P

WMAX = 2
SPAN = 2 * WMAX + 1
R = 3
PICKS = SPAN + R
BLK = 128
BLK_DEV = 6
ROWS = BLK * BLK_DEV
GMAX = 32
G = 128
HD = 128
HEADS_DEV = 2
WIDTH = HD * HEADS_DEV
N_SEQ = 16
N_HEADS = 16
NBLK = N_SEQ * BLK_DEV
UNIT = ROWS + GMAX
NEGATIVE = -1e30
SCALE = 1.0 / math.sqrt(HD)
F32 = jnp.float32
BF16 = jnp.bfloat16

HEAD_SLOTS = (
    ((0, 0), (0, 0), (0, 0)),
    ((-1, 0), (1, 0), (-1, 0)),
    ((-2, 0), (2, 0), (2, 0)),
    ((-3, 0), (2, 1), (-2, 0)),
    ((-2, 1), (3, 1), (1, 0)),
)
Z_UP = [(h, (h + 2) % 16) for h in range(16)]
Z_DOWN = [(h, (h - 2) % 16) for h in range(16)]
PAIR = [(h, h ^ 1) for h in range(16)]


def head_order():
    items = [(0, 0)]
    for up, down, across in HEAD_SLOTS:
        items += [
            (up[0] - 1, up[1]),
            (down[0] + 1, down[1]),
            (across[0], across[1] ^ 1),
        ]
    return items


Y_UP = [(s, (s // 8) * 8 + (s % 8 + 2) % 8) for s in range(16)]
Y_DOWN = [(s, (s // 8) * 8 + (s % 8 - 2) % 8) for s in range(16)]
HALF = [(s, s ^ 8) for s in range(16)]
CORE = [(s, s ^ 1) for s in range(16)]
Y_PAIR = [(s, s ^ 2) for s in range(16)]


def vmem():
    return pl.BlockSpec(memory_space=pltpu.VMEM)


def in_hbm(array):
    return pltpu.with_memory_space_constraint(array, pltpu.HBM)


def project_kernel(count, n_w, first, last, ids, core, *refs):
    xs, refs = refs[:count], refs[count:]
    ws, refs = refs[: n_w * count], refs[n_w * count :]
    if not first:
        acc, refs = refs[0], refs[1:]
    if last:
        sel_ref, ours, theirs = refs
    else:
        (out,) = refs
    parts = []
    for j in range(n_w):
        total = None if first else acc[:, j * WIDTH : (j + 1) * WIDTH]
        for i in range(count):
            term = jnp.dot(xs[i][...], ws[n_w * i + j][...], preferred_element_type=F32)
            total = term if total is None else total + term
        if last:
            parts.append(total.astype(BF16))
        else:
            out[:, j * WIDTH : (j + 1) * WIDTH] = total
    if last:
        columns = lax.broadcasted_iota(jnp.int32, (GMAX, ROWS), 1)
        pick = jnp.where(columns == sel_ref[...], 1.0, 0.0).astype(BF16)
        second = core[0] > 0
        for j, part in enumerate(parts):
            chosen = jnp.dot(pick, part, preferred_element_type=F32).astype(BF16)
            span = slice(j * HD, (j + 1) * HD)
            for rows, have in ((slice(0, ROWS), part), (slice(ROWS, UNIT), chosen)):
                left, right = have[:, :HD], have[:, HD:]
                ours[rows, span] = jnp.where(second, right, left)
                theirs[rows, span] = jnp.where(second, left, right)


def project(ids, core, offset, xs, weights, acc, selected=None):
    count, n_w = len(xs), len(weights)
    first, last = acc is None, selected is not None
    full = lambda shape: pl.BlockSpec(shape, lambda g, ids, core: (0, 0))
    in_specs = [full((ROWS, WIDTH)) for _ in xs]
    operands = list(xs)
    for i in range(count):
        for w in weights:
            in_specs.append(
                pl.BlockSpec(
                    (WIDTH, WIDTH), lambda g, ids, core, i=i: (ids[offset + i], 0)
                )
            )
            operands.append(in_hbm(w))
    aliases = {}
    if not first:
        in_specs.append(full((ROWS, n_w * WIDTH)))
        operands.append(acc)
        if not last:
            aliases = {len(operands) + 1: 0}
    if last:
        in_specs.append(full((GMAX, 1)))
        operands.append(selected)
        out_shape = (jax.ShapeDtypeStruct((UNIT, n_w * HD), BF16),) * 2
        out_specs = (full((UNIT, n_w * HD)),) * 2
    else:
        out_shape = jax.ShapeDtypeStruct((ROWS, n_w * WIDTH), F32)
        out_specs = full((ROWS, n_w * WIDTH))

    def body(*refs):
        project_kernel(count, n_w, first, last, *refs)

    return pl.pallas_call(
        body,
        out_shape=out_shape,
        grid_spec=pltpu.PrefetchScalarGridSpec(
            num_scalar_prefetch=2, grid=(1,), in_specs=in_specs, out_specs=out_specs
        ),
        input_output_aliases=aliases,
        compiler_params=pltpu.CompilerParams(vmem_limit_bytes=40 << 20),
        cost_estimate=pl.CostEstimate(
            flops=2 * count * ROWS * WIDTH * n_w * WIDTH,
            transcendentals=0,
            bytes_accessed=6 << 20,
        ),
        name="project",
    )(ids, core, *operands)


def combine_kernel(count, first, last, ids, odd, *refs):
    cs, refs = refs[:count], refs[count:]
    ws, refs = refs[: 4 * count], refs[4 * count :]
    flip = odd[0] > 0
    total = None
    if not first:
        acc, refs = refs[0], refs[1:]
        total = acc[...]
    (out,) = refs
    for i in range(count):
        quarters = [w[0] for w in ws[4 * i : 4 * i + 4]]
        w = jnp.concatenate(
            [
                jnp.where(flip, quarters[n ^ 1], quarters[n])
                for n in range(4)
            ],
            axis=0,
        )
        part = jnp.dot(cs[i][...], w, preferred_element_type=F32)
        part = part.astype(BF16).astype(F32)
        total = part if total is None else total + part
    out[...] = total.astype(out.dtype)


def combine(ids, odd, offset, cs, w_parts, acc, last=False):
    count = len(cs)
    first = acc is None
    full = lambda shape: pl.BlockSpec(shape, lambda g, ids, odd: (0, 0))
    in_specs = [full((ROWS, WIDTH)) for _ in cs]
    operands = list(cs)
    for i in range(count):
        for w in w_parts:
            in_specs.append(
                pl.BlockSpec(
                    (1, WIDTH // 4, WIDTH),
                    lambda g, ids, odd, i=i: (ids[offset + i], 0, 0),
                )
            )
            operands.append(in_hbm(w))
    aliases = {}
    if not first:
        in_specs.append(full((ROWS, WIDTH)))
        operands.append(acc)
        if not last:
            aliases = {len(operands) + 1: 0}

    def body(*refs):
        combine_kernel(count, first, last, *refs)

    return pl.pallas_call(
        body,
        out_shape=jax.ShapeDtypeStruct((ROWS, WIDTH), BF16 if last else F32),
        grid_spec=pltpu.PrefetchScalarGridSpec(
            num_scalar_prefetch=2,
            grid=(1,),
            in_specs=in_specs,
            out_specs=full((ROWS, WIDTH)),
        ),
        input_output_aliases=aliases,
        compiler_params=pltpu.CompilerParams(vmem_limit_bytes=40 << 20),
        cost_estimate=pl.CostEstimate(
            flops=2 * count * ROWS * WIDTH * WIDTH,
            transcendentals=0,
            bytes_accessed=3 << 20,
        ),
        name="combine",
    )(ids, odd, *operands)


def split_kernel(quarter, w_ref, out_ref):
    for j in range(N_HEADS):
        out_ref[j] = w_ref[:, j * WIDTH : (j + 1) * WIDTH]


def split_columns(quarter, w_out):
    rows = WIDTH // 4
    return pl.pallas_call(
        split_kernel,
        out_shape=jax.ShapeDtypeStruct((N_HEADS, rows, WIDTH), BF16),
        grid_spec=pltpu.PrefetchScalarGridSpec(
            num_scalar_prefetch=1,
            grid=(1,),
            in_specs=[
                pl.BlockSpec(
                    (rows, N_HEADS * WIDTH), lambda g, quarter: (quarter[0], 0)
                )
            ],
            out_specs=pl.BlockSpec(
                (N_HEADS, rows, WIDTH), lambda g, quarter: (0, 0, 0)
            ),
        ),
        cost_estimate=pl.CostEstimate(
            flops=0, transcendentals=0, bytes_accessed=1 << 20
        ),
        name="split_columns",
    )(quarter, in_hbm(w_out))


def gather_heads(own, work):
    have = {(0, 0): own}
    before = [own]
    crossed = []
    state = None
    for t, (up, down, across) in enumerate(HEAD_SLOTS):
        ready = [have[up], have[down], have[across]]
        if state is not None:
            for i in [i for i in range(2) if (i, t) not in ((0, 4), (1, 3))]:
                ready[i] = lax.optimization_barrier((ready[i], state))[0]
        if t > 1:
            ready[2] = lax.optimization_barrier((ready[2], crossed[t - 2]))[0]
        got = [
            lax.ppermute(ready[0], "heads", Z_UP),
            lax.ppermute(ready[1], "heads", Z_DOWN),
            lax.ppermute(ready[2], "heads", PAIR),
        ]
        crossed.append(got[2])
        state = work.state = work(t, before)
        have[(up[0] - 1, up[1])] = got[0]
        have[(down[0] + 1, down[1])] = got[1]
        have[(across[0], across[1] ^ 1)] = got[2]
        before = got
    return before


def gather_seq(mine, theirs):
    up = lambda a: lax.ppermute(a, "seq", Y_UP)
    down = lambda a: lax.ppermute(a, "seq", Y_DOWN)
    half = lambda a: lax.ppermute(a, "seq", HALF)
    near = ({(0, 0): mine}, {(0, 0): theirs})
    for n in near:
        n[1, 0] = half(n[0, 0])
        n[0, 3] = up(n[0, 0])
        n[0, 1] = down(n[0, 0])
    for n in near:
        n[1, 3] = half(n[0, 3])
        n[0, 2] = up(n[0, 3])
        n[1, 1] = down(n[1, 0])
    near[0][1, 2] = up(near[0][1, 3])
    near[1][1, 2] = down(near[1][1, 1])
    return [near[slot % 2][slot // 8, slot // 2 % 4] for slot in range(N_SEQ)]


def attention_kernel(slots, rows, reach, *refs):
    queries, (gslot_ref, *sels), refs = refs[:2], refs[2:5], refs[5:]
    pieces, (*outs, buf, sems) = refs[:N_SEQ], refs[N_SEQ:]
    copies = [
        pltpu.make_async_copy(pieces[i], buf.at[i], sems.at[i]) for i in range(N_SEQ)
    ]
    for copy in copies:
        copy.start()
    for copy in copies:
        copy.wait()

    dims = (((1,), (1,)), ((), ()))

    def scored(q, k):
        return lax.dot_general(q, k, dims, preferred_element_type=F32) * SCALE

    found = jnp.concatenate([buf[i, ROWS:UNIT, :] for i in range(N_SEQ)], axis=0)
    where = lax.broadcasted_iota(jnp.int32, (G, N_SEQ * GMAX), 1)
    pick = jnp.where(where == gslot_ref[...], 1.0, 0.0).astype(BF16)
    g_kv = jnp.dot(pick, found, preferred_element_type=F32).astype(BF16)

    g_query = jnp.concatenate([q[ROWS:UNIT, :] for q in queries], axis=0)
    g_scores = [scored(g_query, buf[i, :ROWS, :HD]) for i in range(N_SEQ)]
    top = g_scores[0]
    for s in g_scores[1:]:
        top = jnp.maximum(top, s)
    top = jnp.max(top, axis=1, keepdims=True)
    sums = jnp.zeros((2 * GMAX, ROWS), F32)
    acc = jnp.zeros((2 * GMAX, HD), F32)
    for i in range(N_SEQ):
        p = jnp.exp(g_scores[i] - top)
        sums = sums + p
        acc = acc + jnp.dot(
            p.astype(BF16), buf[i, :ROWS, HD:], preferred_element_type=F32
        )
    g_context = (acc / jnp.sum(sums, axis=1, keepdims=True)).astype(BF16)

    wide = reach[0] >= WMAX
    for side in range(2):
        steps = lax.broadcasted_iota(jnp.int32, (ROWS, GMAX), 0)
        place = jnp.where(steps == sels[side][...], 1.0, 0.0)
        is_global = jnp.sum(place, axis=1, keepdims=True) > 0.5
        placed = jnp.dot(
            place.astype(BF16),
            g_context[side * GMAX : (side + 1) * GMAX],
            preferred_element_type=F32,
        )
        for b in range(BLK_DEV):
            span = slice(b * BLK, (b + 1) * BLK)
            query = queries[side][span, :]
            first = (side * BLK_DEV + b) * PICKS
            keys_at = [
                (slots[first + j], pl.ds(pl.multiple_of(rows[first + j], BLK), BLK))
                for j in range(PICKS)
            ]
            keys = [buf[slot, at, :HD] for slot, at in keys_at] + [g_kv[:, :HD]]
            values = [buf[slot, at, HD:] for slot, at in keys_at] + [g_kv[:, HD:]]
            scores = scored(query, jnp.concatenate(keys, axis=0))
            scores = [
                jnp.where(wide, scores[:, :BLK], NEGATIVE),
                scores[:, BLK : (SPAN - 1) * BLK],
                jnp.where(wide, scores[:, (SPAN - 1) * BLK : SPAN * BLK], NEGATIVE),
                scores[:, SPAN * BLK :],
            ]
            scores = jnp.concatenate(scores, axis=1)
            top = jnp.max(scores, axis=1, keepdims=True)
            p = jnp.exp(scores - top)
            acc = jnp.dot(
                p.astype(BF16),
                jnp.concatenate(values, axis=0),
                preferred_element_type=F32,
            )
            context = acc / jnp.sum(p, axis=1, keepdims=True)
            outs[side][span, :] = jnp.where(
                is_global[span], placed[span], context
            ).astype(BF16)


def attention(slots, rows, reach, queries, gslot, selected, pieces):
    return pl.pallas_call(
        attention_kernel,
        out_shape=(jax.ShapeDtypeStruct((ROWS, HD), BF16),) * 2,
        grid_spec=pltpu.PrefetchScalarGridSpec(
            num_scalar_prefetch=3,
            grid=(),
            in_specs=[vmem()] * 5
            + [pl.BlockSpec(memory_space=pl.ANY)] * len(pieces),
            out_specs=(vmem(),) * 2,
            scratch_shapes=[
                pltpu.VMEM((N_SEQ, UNIT, 2 * HD), BF16),
                pltpu.SemaphoreType.DMA((len(pieces),)),
            ],
        ),
        compiler_params=pltpu.CompilerParams(vmem_limit_bytes=48 << 20),
        cost_estimate=pl.CostEstimate(
            flops=2 << 30, transcendentals=3 << 20, bytes_accessed=8 << 20
        ),
        name="attention",
    )(slots, rows, reach, *queries, gslot, *selected, *[in_hbm(p) for p in pieces])


def on_device(
    activations, w_query, w_key, w_value, w_out, windows, rand_blocks, global_pos
):
    me = lax.axis_index("heads")
    here = lax.axis_index("seq")
    items = head_order()
    shifts = jnp.array([d for d, _ in items], jnp.int32)
    flips = jnp.array([e for _, e in items], jnp.int32)
    ids = (me // 2 + shifts + 8) % 8 * 2 + (me % 2 + flips) % 2

    def slot_of(seq):
        dx = (seq // 8 + here // 8) % 2
        dy = (seq // 2 % 4 - here // 2 % 4 + 4) % 4
        return dx * 8 + dy * 2 + (seq + here) % 2

    swap = lambda a: lax.ppermute(a, "seq", CORE)
    other = here + 1 - 2 * (here % 2)
    sides = jnp.stack([here, other])
    blocks = (
        sides[:, None] * BLK_DEV + jnp.arange(BLK_DEV, dtype=jnp.int32)[None, :]
    ).reshape(-1, 1)
    offsets = jnp.arange(SPAN, dtype=jnp.int32)[None, :] - WMAX
    near = (blocks + offsets + NBLK) % NBLK
    picks = jnp.concatenate([rand_blocks, swap(rand_blocks)], axis=0)
    named = jnp.concatenate([near, picks], axis=1).reshape(-1)
    key_slots = slot_of(named // BLK_DEV)
    key_rows = named % BLK_DEV * BLK

    owners = global_pos // ROWS
    order = jnp.arange(G, dtype=jnp.int32)
    earlier = (owners[:, None] == owners[None, :]) & (order[None, :] < order[:, None])
    ranks = jnp.sum(earlier.astype(jnp.int32), axis=1)
    gslot = (slot_of(owners) * GMAX + ranks)[:, None]
    local = owners[None, None, :] == sides[:, None, None]
    mine = local & (
        ranks[None, :] == jnp.arange(GMAX, dtype=jnp.int32)[:, None]
    )
    selected = jnp.max(jnp.where(mine, global_pos % ROWS, -1), axis=2)

    weights = (w_key, w_value)
    core = (here % 2)[None]
    odd = (here // 2 % 2)[None]

    shards = []

    class Projection:
        state = None

        def __call__(self, t, arrivals):
            shards.extend(arrivals)
            acc = self.state and self.state[0]
            acc = project(ids, core, max(3 * t - 2, 0), arrivals, weights, acc)
            if t == 1:
                return acc, split_columns(core * 2 + odd, w_out)
            return (acc, *self.state[1:]) if self.state else (acc,)

    projection = Projection()
    last = gather_heads(activations, projection)
    acc, w_blocks = projection.state
    kv, kv_away = project(
        ids, core, 13, last, weights, acc, selected=selected[0][:, None]
    )
    query, query_away = project(
        ids,
        core,
        0,
        [*shards, *last],
        (w_query,),
        None,
        selected=selected[0][:, None],
    )
    pieces = gather_seq(kv, swap(kv_away))
    query_here = swap(query_away)
    pieces[6], w_blocks = lax.optimization_barrier((pieces[6], w_blocks))
    w_quarter = lax.all_to_all(w_blocks, "heads", 0, 0)
    pieces, w_quarter = lax.optimization_barrier((pieces, w_quarter))
    w_half = (w_quarter, lax.ppermute(w_quarter, "seq", Y_PAIR))
    context, context_away = attention(
        key_slots,
        key_rows,
        jnp.where(core > 0, windows[1:], windows[:1]),
        (query, query_here),
        gslot,
        (selected[:1], selected[1:]),
        pieces,
    )
    context = jnp.concatenate([context, swap(context_away)], axis=1)
    context, w_half = lax.optimization_barrier((context, w_half))
    w_parts = (*w_half, *(swap(w) for w in w_half))

    class Combination:
        state = None
        waiting = ()

        def __call__(self, t, arrivals):
            self.waiting = (*self.waiting, *arrivals)
            if t < 2:
                return self.state
            start = 3 * t + 1 - len(self.waiting)
            out = combine(
                ids, odd, start, self.waiting, w_parts, self.state, last=t == 5
            )
            self.waiting = ()
            return out

    combination = Combination()
    return combination(5, gather_heads(context, combination))


def solution(mesh):
    in_specs = (
        P("seq", "heads"),
        P(None, "heads"),
        P(None, "heads"),
        P(None, "heads"),
        P("heads", None),
        P("heads"),
        P("seq", None),
        P(),
    )
    out_specs = P("seq", "heads")
    return jax.shard_map(
        on_device, mesh=mesh, in_specs=in_specs, out_specs=out_specs, check_vma=False
    )
```

```python
import math

import jax
import jax.numpy as jnp
from jax import lax
from jax.experimental import pallas as pl
from jax.experimental.pallas import tpu as pltpu
from jax.sharding import PartitionSpec as P

WMAX = 2
SPAN = 2 * WMAX + 1
R = 3
PICKS = SPAN + R
BLK = 128
BLK_DEV = 6
ROWS = BLK * BLK_DEV
GMAX = 32
G = 128
HD = 128
HEADS_DEV = 2
WIDTH = HD * HEADS_DEV
N_SEQ = 16
N_HEADS = 16
NBLK = N_SEQ * BLK_DEV
UNIT = ROWS + GMAX
NEGATIVE = -1e30
SCALE = 1.0 / math.sqrt(HD)
F32 = jnp.float32
BF16 = jnp.bfloat16

HEAD_SLOTS = (
    ((0, 0), (0, 0), (0, 0)),
    ((-1, 0), (1, 0), (-1, 0)),
    ((-2, 0), (2, 0), (1, 0)),
    ((-3, 0), (1, 1), (-2, 0)),
    ((-2, 1), (2, 1), (-4, 0)),
)
Z_UP = [(h, (h + 2) % 16) for h in range(16)]
Z_DOWN = [(h, (h - 2) % 16) for h in range(16)]
PAIR = [(h, h ^ 1) for h in range(16)]


def head_order():
    items = [(0, 0)]
    for up, down, across in HEAD_SLOTS:
        items += [
            (up[0] - 1, up[1]),
            (down[0] + 1, down[1]),
            (across[0], across[1] ^ 1),
        ]
    return items


Y_UP = [(s, (s // 8) * 8 + (s % 8 + 2) % 8) for s in range(16)]
Y_DOWN = [(s, (s // 8) * 8 + (s % 8 - 2) % 8) for s in range(16)]
HALF = [(s, s ^ 8) for s in range(16)]
CORE = [(s, s ^ 1) for s in range(16)]
Y_PAIR = [(s, s ^ 2) for s in range(16)]


def vmem():
    return pl.BlockSpec(memory_space=pltpu.VMEM)


def in_hbm(array):
    return pltpu.with_memory_space_constraint(array, pltpu.HBM)


def project_kernel(count, first, last, ids, core, *refs):
    xs, refs = refs[:count], refs[count:]
    ws, refs = refs[: 3 * count], refs[3 * count :]
    if not first:
        acc, refs = refs[0], refs[1:]
    if last:
        sel_ref, *outs = refs
    else:
        (out,) = refs
    parts = []
    for j in range(3):
        total = None if first else acc[:, j * WIDTH : (j + 1) * WIDTH]
        for i in range(count):
            term = jnp.dot(
                xs[i][...], ws[3 * i + j][...], preferred_element_type=F32
            )
            total = term if total is None else total + term
        if last:
            parts.append(total.astype(BF16))
        else:
            out[:, j * WIDTH : (j + 1) * WIDTH] = total
    if last:
        columns = lax.broadcasted_iota(jnp.int32, (GMAX, ROWS), 1)
        pick = jnp.where(columns == sel_ref[...], 1.0, 0.0).astype(BF16)
        second = core[0] > 0
        for j, part in enumerate(parts):
            chosen = jnp.dot(pick, part, preferred_element_type=F32).astype(BF16)
            low = max(j - 1, 0) * HD
            for rows, have in ((slice(0, ROWS), part), (slice(ROWS, UNIT), chosen)):
                left, right = have[:, :HD], have[:, HD:]
                q_or_kv = outs[:2] if j == 0 else outs[2:]
                q_or_kv[0][rows, low : low + HD] = jnp.where(second, right, left)
                q_or_kv[1][rows, low : low + HD] = jnp.where(second, left, right)


def project(ids, core, offset, xs, weights, acc, selected=None):
    count = len(xs)
    first, last = acc is None, selected is not None
    full = lambda shape: pl.BlockSpec(shape, lambda g, ids, core: (0, 0))
    in_specs = [full((ROWS, WIDTH)) for _ in xs]
    operands = list(xs)
    for i in range(count):
        for w in weights:
            in_specs.append(
                pl.BlockSpec((WIDTH, WIDTH), lambda g, ids, core, i=i: (ids[offset + i], 0))
            )
            operands.append(in_hbm(w))
    aliases = {}
    if not first:
        in_specs.append(full((ROWS, 3 * WIDTH)))
        operands.append(acc)
        if not last:
            aliases = {len(operands) + 1: 0}
    if last:
        in_specs.append(full((GMAX, 1)))
        operands.append(selected)
        shapes = ((UNIT, HD),) * 2 + ((UNIT, 2 * HD),) * 2
        out_shape = tuple(jax.ShapeDtypeStruct(shape, BF16) for shape in shapes)
        out_specs = tuple(full(shape) for shape in shapes)
    else:
        out_shape = jax.ShapeDtypeStruct((ROWS, 3 * WIDTH), F32)
        out_specs = full((ROWS, 3 * WIDTH))

    def body(*refs):
        project_kernel(count, first, last, *refs)

    return pl.pallas_call(
        body,
        out_shape=out_shape,
        grid_spec=pltpu.PrefetchScalarGridSpec(
            num_scalar_prefetch=2, grid=(1,), in_specs=in_specs, out_specs=out_specs
        ),
        input_output_aliases=aliases,
        compiler_params=pltpu.CompilerParams(vmem_limit_bytes=40 << 20),
        cost_estimate=pl.CostEstimate(
            flops=2 * count * ROWS * WIDTH * 3 * WIDTH,
            transcendentals=0,
            bytes_accessed=6 << 20,
        ),
        name="project",
    )(ids, core, *operands)


def combine_kernel(count, first, last, ids, odd, *refs):
    cs, refs = refs[:count], refs[count:]
    ws, refs = refs[: 4 * count], refs[4 * count :]
    flip = odd[0] > 0
    total = None
    if not first:
        acc, refs = refs[0], refs[1:]
        total = acc[...]
    (out,) = refs
    for i in range(count):
        quarters = [w[0] for w in ws[4 * i : 4 * i + 4]]
        w = jnp.concatenate(
            [
                jnp.where(flip, quarters[n ^ 1], quarters[n])
                for n in range(4)
            ],
            axis=0,
        )
        part = jnp.dot(cs[i][...], w, preferred_element_type=F32)
        part = part.astype(BF16).astype(F32)
        total = part if total is None else total + part
    out[...] = total.astype(out.dtype)


def combine(ids, odd, offset, cs, w_parts, acc, last=False):
    count = len(cs)
    first = acc is None
    full = lambda shape: pl.BlockSpec(shape, lambda g, ids, odd: (0, 0))
    in_specs = [full((ROWS, WIDTH)) for _ in cs]
    operands = list(cs)
    for i in range(count):
        for w in w_parts:
            in_specs.append(
                pl.BlockSpec(
                    (1, WIDTH // 4, WIDTH),
                    lambda g, ids, odd, i=i: (ids[offset + i], 0, 0),
                )
            )
            operands.append(in_hbm(w))
    aliases = {}
    if not first:
        in_specs.append(full((ROWS, WIDTH)))
        operands.append(acc)
        if not last:
            aliases = {len(operands) + 1: 0}

    def body(*refs):
        combine_kernel(count, first, last, *refs)

    return pl.pallas_call(
        body,
        out_shape=jax.ShapeDtypeStruct((ROWS, WIDTH), BF16 if last else F32),
        grid_spec=pltpu.PrefetchScalarGridSpec(
            num_scalar_prefetch=2,
            grid=(1,),
            in_specs=in_specs,
            out_specs=full((ROWS, WIDTH)),
        ),
        input_output_aliases=aliases,
        compiler_params=pltpu.CompilerParams(vmem_limit_bytes=40 << 20),
        cost_estimate=pl.CostEstimate(
            flops=2 * count * ROWS * WIDTH * WIDTH,
            transcendentals=0,
            bytes_accessed=3 << 20,
        ),
        name="combine",
    )(ids, odd, *operands)


def split_kernel(quarter, w_ref, out_ref):
    for j in range(N_HEADS):
        out_ref[j] = w_ref[:, j * WIDTH : (j + 1) * WIDTH]


def split_columns(quarter, w_out):
    rows = WIDTH // 4
    return pl.pallas_call(
        split_kernel,
        out_shape=jax.ShapeDtypeStruct((N_HEADS, rows, WIDTH), BF16),
        grid_spec=pltpu.PrefetchScalarGridSpec(
            num_scalar_prefetch=1,
            grid=(1,),
            in_specs=[
                pl.BlockSpec(
                    (rows, N_HEADS * WIDTH), lambda g, quarter: (quarter[0], 0)
                )
            ],
            out_specs=pl.BlockSpec(
                (N_HEADS, rows, WIDTH), lambda g, quarter: (0, 0, 0)
            ),
        ),
        cost_estimate=pl.CostEstimate(
            flops=0, transcendentals=0, bytes_accessed=1 << 20
        ),
        name="split_columns",
    )(quarter, in_hbm(w_out))


def gather_heads(own, work):
    have = {(0, 0): own}
    before = [own]
    state = None
    for t, (up, down, across) in enumerate(HEAD_SLOTS):
        ready = [have[up], have[down], have[across]]
        if state is not None:
            ready = [lax.optimization_barrier((item, state))[0] for item in ready]
        got = [
            lax.ppermute(ready[0], "heads", Z_UP),
            lax.ppermute(ready[1], "heads", Z_DOWN),
            lax.ppermute(ready[2], "heads", PAIR),
        ]
        state = work.state = work(t, before)
        have[(up[0] - 1, up[1])] = got[0]
        have[(down[0] + 1, down[1])] = got[1]
        have[(across[0], across[1] ^ 1)] = got[2]
        before = got
    return before


def gather_seq(mine, theirs):
    up = lambda a: lax.ppermute(a, "seq", Y_UP)
    down = lambda a: lax.ppermute(a, "seq", Y_DOWN)
    half = lambda a: lax.ppermute(a, "seq", HALF)
    near = ({(0, 0): mine}, {(0, 0): theirs})
    for n in near:
        n[1, 0] = half(n[0, 0])
        n[0, 3] = up(n[0, 0])
        n[0, 1] = down(n[0, 0])
    for n in near:
        n[1, 3] = half(n[0, 3])
        n[0, 2] = up(n[0, 3])
        n[1, 1] = down(n[1, 0])
    near[0][1, 2] = up(near[0][1, 3])
    near[1][1, 2] = down(near[1][1, 1])
    return [near[slot % 2][slot // 8, slot // 2 % 4] for slot in range(N_SEQ)]


def attention_kernel(slots, rows, reach, *refs):
    queries, (gslot_ref, *sels), refs = refs[:2], refs[2:5], refs[5:]
    pieces, (*outs, buf, sems) = refs[:N_SEQ], refs[N_SEQ:]
    copies = [
        pltpu.make_async_copy(pieces[i], buf.at[i], sems.at[i]) for i in range(N_SEQ)
    ]
    for copy in copies:
        copy.start()
    for copy in copies:
        copy.wait()

    dims = (((1,), (1,)), ((), ()))

    def scored(q, k):
        return lax.dot_general(q, k, dims, preferred_element_type=F32) * SCALE

    found = jnp.concatenate([buf[i, ROWS:UNIT, :] for i in range(N_SEQ)], axis=0)
    where = lax.broadcasted_iota(jnp.int32, (G, N_SEQ * GMAX), 1)
    pick = jnp.where(where == gslot_ref[...], 1.0, 0.0).astype(BF16)
    g_kv = jnp.dot(pick, found, preferred_element_type=F32).astype(BF16)

    g_query = jnp.concatenate([q[ROWS:UNIT, :] for q in queries], axis=0)
    g_scores = [scored(g_query, buf[i, :ROWS, :HD]) for i in range(N_SEQ)]
    top = g_scores[0]
    for s in g_scores[1:]:
        top = jnp.maximum(top, s)
    top = jnp.max(top, axis=1, keepdims=True)
    sums = jnp.zeros((2 * GMAX, ROWS), F32)
    acc = jnp.zeros((2 * GMAX, HD), F32)
    for i in range(N_SEQ):
        p = jnp.exp(g_scores[i] - top)
        sums = sums + p
        acc = acc + jnp.dot(
            p.astype(BF16), buf[i, :ROWS, HD:], preferred_element_type=F32
        )
    g_context = (acc / jnp.sum(sums, axis=1, keepdims=True)).astype(BF16)

    wide = reach[0] >= WMAX
    for side in range(2):
        steps = lax.broadcasted_iota(jnp.int32, (ROWS, GMAX), 0)
        place = jnp.where(steps == sels[side][...], 1.0, 0.0)
        is_global = jnp.sum(place, axis=1, keepdims=True) > 0.5
        placed = jnp.dot(
            place.astype(BF16),
            g_context[side * GMAX : (side + 1) * GMAX],
            preferred_element_type=F32,
        )
        for b in range(BLK_DEV):
            span = slice(b * BLK, (b + 1) * BLK)
            query = queries[side][span, :]
            first = (side * BLK_DEV + b) * PICKS
            keys_at = [
                (slots[first + j], pl.ds(pl.multiple_of(rows[first + j], BLK), BLK))
                for j in range(PICKS)
            ]
            keys = [buf[slot, at, :HD] for slot, at in keys_at] + [g_kv[:, :HD]]
            values = [buf[slot, at, HD:] for slot, at in keys_at] + [g_kv[:, HD:]]
            scores = scored(query, jnp.concatenate(keys, axis=0))
            scores = [
                jnp.where(wide, scores[:, :BLK], NEGATIVE),
                scores[:, BLK : (SPAN - 1) * BLK],
                jnp.where(wide, scores[:, (SPAN - 1) * BLK : SPAN * BLK], NEGATIVE),
                scores[:, SPAN * BLK :],
            ]
            scores = jnp.concatenate(scores, axis=1)
            top = jnp.max(scores, axis=1, keepdims=True)
            p = jnp.exp(scores - top)
            acc = jnp.dot(
                p.astype(BF16),
                jnp.concatenate(values, axis=0),
                preferred_element_type=F32,
            )
            context = acc / jnp.sum(p, axis=1, keepdims=True)
            outs[side][span, :] = jnp.where(
                is_global[span], placed[span], context
            ).astype(BF16)


def attention(slots, rows, reach, queries, gslot, selected, pieces):
    return pl.pallas_call(
        attention_kernel,
        out_shape=(jax.ShapeDtypeStruct((ROWS, HD), BF16),) * 2,
        grid_spec=pltpu.PrefetchScalarGridSpec(
            num_scalar_prefetch=3,
            grid=(),
            in_specs=[vmem()] * 5
            + [pl.BlockSpec(memory_space=pl.ANY)] * len(pieces),
            out_specs=(vmem(),) * 2,
            scratch_shapes=[
                pltpu.VMEM((N_SEQ, UNIT, 2 * HD), BF16),
                pltpu.SemaphoreType.DMA((len(pieces),)),
            ],
        ),
        compiler_params=pltpu.CompilerParams(vmem_limit_bytes=48 << 20),
        cost_estimate=pl.CostEstimate(
            flops=2 << 30, transcendentals=3 << 20, bytes_accessed=8 << 20
        ),
        name="attention",
    )(slots, rows, reach, *queries, gslot, *selected, *[in_hbm(p) for p in pieces])


def on_device(
    activations, w_query, w_key, w_value, w_out, windows, rand_blocks, global_pos
):
    me = lax.axis_index("heads")
    here = lax.axis_index("seq")
    items = head_order()
    shifts = jnp.array([d for d, _ in items], jnp.int32)
    flips = jnp.array([e for _, e in items], jnp.int32)
    ids = (me // 2 + shifts + 8) % 8 * 2 + (me % 2 + flips) % 2

    def slot_of(seq):
        dx = (seq // 8 + here // 8) % 2
        dy = (seq // 2 % 4 - here // 2 % 4 + 4) % 4
        return dx * 8 + dy * 2 + (seq + here) % 2

    swap = lambda a: lax.ppermute(a, "seq", CORE)
    other = here + 1 - 2 * (here % 2)
    sides = jnp.stack([here, other])
    blocks = (
        sides[:, None] * BLK_DEV + jnp.arange(BLK_DEV, dtype=jnp.int32)[None, :]
    ).reshape(-1, 1)
    offsets = jnp.arange(SPAN, dtype=jnp.int32)[None, :] - WMAX
    near = (blocks + offsets + NBLK) % NBLK
    picks = jnp.concatenate([rand_blocks, swap(rand_blocks)], axis=0)
    named = jnp.concatenate([near, picks], axis=1).reshape(-1)
    key_slots = slot_of(named // BLK_DEV)
    key_rows = named % BLK_DEV * BLK

    owners = global_pos // ROWS
    order = jnp.arange(G, dtype=jnp.int32)
    earlier = (owners[:, None] == owners[None, :]) & (order[None, :] < order[:, None])
    ranks = jnp.sum(earlier.astype(jnp.int32), axis=1)
    gslot = (slot_of(owners) * GMAX + ranks)[:, None]
    local = owners[None, None, :] == sides[:, None, None]
    mine = local & (
        ranks[None, :] == jnp.arange(GMAX, dtype=jnp.int32)[:, None]
    )
    selected = jnp.max(jnp.where(mine, global_pos % ROWS, -1), axis=2)

    weights = (w_query, w_key, w_value)
    core = (here % 2)[None]
    odd = (here // 2 % 2)[None]

    class Projection:
        state = None

        def __call__(self, t, arrivals):
            acc = self.state and self.state[0]
            acc = project(ids, core, max(3 * t - 2, 0), arrivals, weights, acc)
            if t == 1:
                return acc, split_columns(core * 2 + odd, w_out)
            return (acc, *self.state[1:]) if self.state else (acc,)

    projection = Projection()
    last = gather_heads(activations, projection)
    acc, w_blocks = projection.state
    query, query_away, kv, kv_away = project(
        ids, core, 13, last, weights, acc, selected=selected[0][:, None]
    )
    query_here, w_blocks = lax.optimization_barrier((swap(query_away), w_blocks))
    w_quarter = lax.all_to_all(w_blocks, "heads", 0, 0)
    pieces = gather_seq(kv, swap(kv_away))
    pieces, w_quarter = lax.optimization_barrier((pieces, w_quarter))
    w_half = (w_quarter, lax.ppermute(w_quarter, "seq", Y_PAIR))
    context, context_away = attention(
        key_slots,
        key_rows,
        jnp.where(core > 0, windows[1:], windows[:1]),
        (query, query_here),
        gslot,
        (selected[:1], selected[1:]),
        pieces,
    )
    context = jnp.concatenate([context, swap(context_away)], axis=1)
    context, w_half = lax.optimization_barrier((context, w_half))
    w_parts = (*w_half, *(swap(w) for w in w_half))

    class Combination:
        state = None
        waiting = ()

        def __call__(self, t, arrivals):
            self.waiting = (*self.waiting, *arrivals)
            if t < 2:
                return self.state
            start = 3 * t + 1 - len(self.waiting)
            out = combine(
                ids, odd, start, self.waiting, w_parts, self.state, last=t == 5
            )
            self.waiting = ()
            return out

    combination = Combination()
    return combination(5, gather_heads(context, combination))


def solution(mesh):
    in_specs = (
        P("seq", "heads"),
        P(None, "heads"),
        P(None, "heads"),
        P(None, "heads"),
        P("heads", None),
        P("heads"),
        P("seq", None),
        P(),
    )
    out_specs = P("seq", "heads")
    return jax.shard_map(
        on_device, mesh=mesh, in_specs=in_specs, out_specs=out_specs, check_vma=False
    )
```
